512 devices in a mesh: node: 32 (over z_lo, x, core), group: 16 (over y, z_hi).
Axes of the slice: x: 4, y: 8, z: 8 (z_hi: 2, z_lo: 4; z = z_hi * 4 + z_lo), core: 2. Of those that a mesh axis runs over, the one named last changes fastest.
Arguments:
- tokens: bfloat16 [131072, 1024], P(('node', 'group')), may hold values from -6 to 6
- grad_out: bfloat16 [131072, 1024], P(('node', 'group')), may hold values from -1.5 to 1.5
- router_gate: float32 [131072, 4], P(('node', 'group')), may hold values from 0.1 to 1
- counts: int32 [512], P(('node', 'group')), may hold values from 1 to 2
- routes: int32 [512, 2, 4], P(('node', 'group')), may hold values from 0 to 15, as said below
- partner: int32 [32], replicated, may hold values from 0 to 31, as said below
- w_gate: bfloat16 [512, 1024, 256], P(('node', 'group')), may hold values from -0.1875 to 0.1875
- w_up: bfloat16 [512, 1024, 256], P(('node', 'group')), may hold values from -0.1875 to 0.1875
- w_down: bfloat16 [512, 256, 1024], P(('node', 'group')), may hold values from -0.375 to 0.375
Outputs:
- grad_tokens: bfloat16 [131072, 1024], P(('node', 'group'))
- grad_gate: bfloat16 [512, 1024, 256], P(('node', 'group'))
- grad_up: bfloat16 [512, 1024, 256], P(('node', 'group'))
- grad_down: bfloat16 [512, 256, 1024], P(('node', 'group'))
The draws below stay inside these ranges and needn't reach their ends.
Inputs may be any that keep to these rules, and one draw needn't show every extreme that they name: `routes`: the 8 entries of one device name different devices of its group; every device of a group is named; in every node group one device is named by exactly 12 entries and none by more. partner pairs the nodes: partner[partner[n]] = n and partner[n] != n.
All inputs are finite; a program needn't handle non-finite values.
Results may differ from the reference program's by a relative error of at most 0.015.
Values may be sent and summed in bfloat16 or wider, within the bound.
A program may use at most 128 MiB of HBM per device.

```python
import math
import jax
import jax.numpy as jnp
from jax import lax

D = 1024
H = 256
BLK = 128
NB = 2
TOPK = 4
MAXR = 12
EXPERTS = 512
ROWS = 131072
N_NODE = 32
N_GROUP = 16


def draw_routes(key, part):
    spread = NB * TOPK
    extra = MAXR - spread
    keys = jax.random.split(key, N_NODE)

    def one_group(subkey):
        first_key, second_key, third_key = jax.random.split(subkey, 3)
        start = jax.random.permutation(first_key, N_GROUP).astype(jnp.int32)
        offsets = jnp.arange(spread, dtype=jnp.int32)
        table = ((start[:, None] + offsets[None, :]) % N_GROUP).astype(jnp.int32)
        hottest = jax.random.randint(second_key, (), 0, N_GROUP).astype(jnp.int32)
        names_hot = jnp.any(table == hottest, axis=1).astype(jnp.int32)
        ranks = jax.random.permutation(third_key, N_GROUP).astype(jnp.int32)
        order = jnp.argsort(names_hot * N_GROUP + ranks).astype(jnp.int32)
        picked = jnp.zeros((N_GROUP,), jnp.int32).at[order[:extra]].set(1)
        final = jnp.where(picked == 1, hottest, table[:, spread - 1]).astype(jnp.int32)
        table = table.at[:, spread - 1].set(final)
        return table.reshape(N_GROUP, NB, TOPK)
    return jax.vmap(one_group)(keys).reshape(N_NODE * N_GROUP, NB, TOPK).astype(jnp.int32)


def draw_partner(key, part):
    order = jax.random.permutation(key, N_NODE).astype(jnp.int32)
    mates = order.reshape(N_NODE // 2, 2)[:, ::-1].reshape(N_NODE)
    return jnp.zeros((N_NODE,), jnp.int32).at[order].set(mates)


def touch_ends(array, key, low, top_value):
    spot = [jax.random.randint(jax.random.fold_in(key, axis), (), 0, length) for axis, length in enumerate(array.shape)]
    main_axis = array.shape.index(max(array.shape))
    next_to = spot[:main_axis] + [(spot[main_axis] + 1) % array.shape[main_axis]] + spot[main_axis + 1:]
    return array.at[tuple(spot)].set(low).at[tuple(next_to)].set(top_value)


def block_scale(own_key, extent, cuts, smallest, high):
    def one(axis_at, shards_of):
        draws = jax.random.uniform(jax.random.fold_in(jax.random.fold_in(own_key, 6), axis_at), (shards_of,), jnp.float32, smallest / len(cuts), high / len(cuts))
        return jnp.repeat(jnp.exp(draws), extent[axis_at] // shards_of).reshape((-1,) + (1,) * (len(extent) - axis_at - 1))

    factor_of = one(*cuts[0])
    for cut in cuts[1:]:
        factor_of = factor_of * one(*cut)
    return factor_of


def bell_draw(key, extent, scale, limit, shards=(), kind=jnp.bfloat16):
    loudness = block_scale(key, extent, shards, -0.22, 0.18) if shards else 1.0
    array = jax.random.normal(key, extent, jnp.float32) * scale * loudness
    return jnp.minimum(jnp.maximum(array, -limit), limit).astype(kind)


def setup_inputs(seed: int = 0) -> dict:
    seeds = jax.random.split(jax.random.key(seed), 10)
    tokens = bell_draw(seeds[0], (ROWS, D), 1.0, 6.0, ((0, 512),))
    grad_out = bell_draw(seeds[1], (ROWS, D), 0.25, 1.5, ((0, 512),))
    router_gate = jnp.clip(jnp.exp(math.log(1.0) - 2.3025851 * jax.random.uniform(seeds[2], (ROWS, TOPK), jnp.float32) ** block_scale(seeds[2], (ROWS, TOPK), ((0, 512),), -0.2, 0.2)), 0.1, 1.0)
    counts = touch_ends(jax.random.randint(seeds[3], (EXPERTS,), 1, NB + 1), jax.random.fold_in(seeds[3], 1), 1, NB).astype(jnp.int32)
    routes = draw_routes(jax.random.fold_in(seeds[9], 71), 0)
    partner = draw_partner(jax.random.fold_in(seeds[9], 71), 0)
    w_gate = bell_draw(seeds[6], (EXPERTS, D, H), D ** -0.5, 0.1875, ((0, 512),))
    w_up = bell_draw(seeds[7], (EXPERTS, D, H), D ** -0.5, 0.1875, ((0, 512),))
    w_down = bell_draw(seeds[8], (EXPERTS, H, D), H ** -0.5, 0.375, ((0, 512),))
    return {"tokens": tokens, "grad_out": grad_out, "router_gate": router_gate, "counts": counts, "routes": routes, "partner": partner, "w_gate": w_gate, "w_up": w_up, "w_down": w_down}


def against(left, right):
    return lax.dot_general(left, right, (((1,), (1,)), ((), ())), preferred_element_type=jnp.float32)


def across(left, right):
    return lax.dot_general(left, right, (((0,), (0,)), ((), ())), preferred_element_type=jnp.float32)


def expert_pass(rows, grads, w_gate, w_up, w_down):
    gate_pre = jnp.dot(rows, w_gate, preferred_element_type=jnp.float32)
    up_pre = jnp.dot(rows, w_up, preferred_element_type=jnp.float32)
    sigmoid = jax.nn.sigmoid(gate_pre)
    swish = gate_pre * sigmoid
    hidden = (swish * up_pre).astype(jnp.bfloat16)
    grad_hidden = against(grads, w_down)
    grad_upre = (grad_hidden * swish).astype(jnp.bfloat16)
    grad_gpre = (grad_hidden * up_pre * sigmoid * (1.0 + gate_pre * (1.0 - sigmoid))).astype(jnp.bfloat16)
    back = (against(grad_gpre, w_gate) + against(grad_upre, w_up)).astype(jnp.bfloat16)
    return (back, across(rows, grad_gpre).astype(jnp.bfloat16),
            across(rows, grad_upre).astype(jnp.bfloat16), across(hidden, grads).astype(jnp.bfloat16))


def reference(tokens, grad_out, router_gate, counts, routes, partner, w_gate, w_up, w_down):
    live = jnp.arange(NB)[None, :] < counts[:, None]
    live_rows = jnp.repeat(live, BLK, axis=1).reshape(ROWS)
    masked_tok = jnp.where(live_rows[:, None], tokens, jnp.zeros_like(tokens))
    masked_out = jnp.where(live_rows[:, None], grad_out, jnp.zeros_like(grad_out))
    tok_nodes = masked_tok.reshape(N_NODE, N_GROUP * NB, BLK, D)
    out_nodes = masked_out.reshape(N_NODE, N_GROUP * NB, BLK, D)
    gate_nodes = router_gate.reshape(N_NODE, N_GROUP * NB, BLK, TOPK)
    route_nodes = routes.reshape(N_NODE, N_GROUP * NB * TOPK)
    placed_gate = jnp.take(w_gate.reshape(N_NODE, N_GROUP, D, H), partner, axis=0)
    placed_up = jnp.take(w_up.reshape(N_NODE, N_GROUP, D, H), partner, axis=0)
    placed_down = jnp.take(w_down.reshape(N_NODE, N_GROUP, H, D), partner, axis=0)

    def per_node(packed):
        tok_g, out_g, gate_g, route_g, wg_g, wu_g, wd_g = packed

        def per_expert(expert, wg, wu, wd):
            chosen = route_g == expert
            index = jnp.argsort(jnp.where(chosen, 0, 1).astype(jnp.int32), stable=True)[:MAXR].astype(jnp.int32)
            valid = chosen[index]
            blocks = (index // TOPK).astype(jnp.int32)
            column = (index % TOPK).astype(jnp.int32)
            keep = valid[:, None, None]
            rows = jnp.where(keep, tok_g[blocks], jnp.zeros((), jnp.bfloat16)).reshape(MAXR * BLK, D)
            weight = gate_g[blocks, :, column]
            grads = (weight[:, :, None] * out_g[blocks].astype(jnp.float32)).astype(jnp.bfloat16)
            grads = jnp.where(keep, grads, jnp.zeros((), jnp.bfloat16)).reshape(MAXR * BLK, D)
            back, grad_wg, grad_wu, grad_wd = expert_pass(rows, grads, wg, wu, wd)
            back = jnp.where(keep, back.reshape(MAXR, BLK, D).astype(jnp.float32), jnp.float32(0.0))
            return back, blocks, grad_wg, grad_wu, grad_wd

        back, blocks, grad_wg, grad_wu, grad_wd = jax.vmap(per_expert)(
            jnp.arange(N_GROUP, dtype=jnp.int32), wg_g, wu_g, wd_g)
        total = jnp.zeros((N_GROUP * NB, BLK, D), jnp.float32).at[blocks.reshape(-1)].add(back.reshape(-1, BLK, D))
        return total.astype(jnp.bfloat16), grad_wg, grad_wu, grad_wd

    back, grad_wg, grad_wu, grad_wd = lax.map(
        per_node, (tok_nodes, out_nodes, gate_nodes, route_nodes, placed_gate, placed_up, placed_down))
    back = back.reshape(ROWS, D)
    grad_tokens = jnp.where(live_rows[:, None], back, jnp.zeros_like(back))
    return (grad_tokens, grad_wg.reshape(EXPERTS, D, H), grad_wu.reshape(EXPERTS, D, H),
            grad_wd.reshape(EXPERTS, H, D))
```

```python
import functools

import jax
import jax.numpy as jnp
from jax import lax
from jax.experimental import pallas as pl
from jax.experimental.pallas import tpu as pltpu
from jax.sharding import PartitionSpec as P

BF = jnp.bfloat16
F32 = jnp.float32
MESH = pl.DeviceIdType.MESH
NODES = 32
GROUP = 16
RING = 8
BLK = 128
D = 1024
H = 256
HALF = D // 2
PART = 96


def slot(hops, way):
    if hops == 0:
        return 0
    return 7 if hops == RING // 2 else 2 * hops - 1 + way


def nt(left, right):
    return lax.dot_general(left, right, (((1,), (1,)), ((), ())), preferred_element_type=F32)


def tn(left, right):
    return lax.dot_general(left, right, (((0,), (0,)), ((), ())), preferred_element_type=F32)


def kernel(
    partner, meta_in, tok_in, gr_in, wg_in, wu_in, wd_in,
    dt_out, dg_out, du_out, dd_out,
    meta, tok, gr, xs, gs, gact, hact, cbuf, rbuf, sbuf, zsend, zrecv,
    pack, mixed, stage, wrec, dg_v, du_v, dd_v, dt_v,
    g_send, g_recv, m_send, m_recv, wa_send, wa_recv, wb_send, wb_recv,
    rs_send, rs_recv, z_send, z_recv, loc, out_sem,
):
    n = lax.axis_index("node")
    me = lax.axis_index("group")
    y = me // 2
    side = me % 2
    ring = (lax.rem(y + 1, RING) * 2 + side, lax.rem(y + RING - 1, RING) * 2 + side)
    mate = y * 2 + (1 - side)

    locals_ = [
        pltpu.make_async_copy(wg_in, pack.at[:, :, pl.ds(0, 32), :], loc.at[0]),
        pltpu.make_async_copy(wu_in, pack.at[:, :, pl.ds(32, 32), :], loc.at[1]),
    ]
    for cb in range(4):
        locals_.append(
            pltpu.make_async_copy(
                wd_in.at[:, :, pl.ds(256 * cb, 256)],
                pack.at[:, cb // 2, pl.ds(64 + 16 * (cb % 2), 16), :],
                loc.at[2 + cb],
            )
        )
    owns = [
        pltpu.make_async_copy(meta_in, meta.at[0], loc.at[6]),
        pltpu.make_async_copy(tok_in, tok.at[0], loc.at[7]),
        pltpu.make_async_copy(gr_in, gr.at[0], loc.at[8]),
    ]
    for c in locals_ + owns:
        c.start()

    barrier = pltpu.get_barrier_semaphore()

    def greet(k, carry):
        pl.semaphore_signal(
            barrier, inc=1, device_id=(lax.rem(n + k, NODES), me), device_id_type=MESH
        )
        return carry

    for g in (ring[0], ring[1], mate):
        pl.semaphore_signal(barrier, inc=1, device_id=(n, g), device_id_type=MESH)
    lax.fori_loop(1, NODES, greet, 0)
    pl.semaphore_wait(barrier, NODES - 1 + 3)

    bufs = (meta, tok, gr)
    ins = (meta_in, tok_in, gr_in)

    def gather(q, way, hops, c):
        src = ins[c] if q == 0 and hops == 1 else bufs[c].at[q * 8 + slot(hops - 1, way)]
        return pltpu.make_async_remote_copy(
            src_ref=src,
            dst_ref=bufs[c].at[q * 8 + slot(hops, way)],
            send_sem=g_send.at[q, way, hops - 1, c],
            recv_sem=g_recv.at[q, way, hops - 1, c],
            device_id=(n, ring[way]),
            device_id_type=MESH,
        )

    def has(way, hops, c):
        return hops < RING // 2 or (c == 2) == (way == 1)

    def to_mate(c):
        return pltpu.make_async_remote_copy(
            src_ref=ins[c],
            dst_ref=bufs[c].at[8],
            send_sem=m_send.at[c],
            recv_sem=m_recv.at[c],
            device_id=(n, mate),
            device_id_type=MESH,
        )

    def spread(k):
        to = lax.rem(n + k, NODES)
        return pltpu.make_async_remote_copy(
            src_ref=pack.at[to // 2, lax.rem(to, 2)],
            dst_ref=mixed.at[n],
            send_sem=wa_send.at[k],
            recv_sem=wa_recv.at[k],
            device_id=(to, me),
            device_id_type=MESH,
        )

    def collect(k):
        to = lax.rem(n + k, NODES)
        return pltpu.make_async_remote_copy(
            src_ref=stage.at[to],
            dst_ref=wrec.at[n],
            send_sem=wb_send.at[k],
            recv_sem=wb_recv.at[k],
            device_id=(to, me),
            device_id_type=MESH,
        )

    def each_peer(act):
        def body(k, carry):
            act(k)
            return carry

        lax.fori_loop(1, NODES, body, 0)

    def arrive(q, hops, c):
        for way in range(2):
            if has(way, hops, c):
                gather(q, way, hops, c).wait_recv()
                if hops < RING // 2 and has(way, hops + 1, c):
                    gather(q, way, hops + 1, c).start()

    def chosen_row(s):
        return meta[s, pl.ds(GROUP + me, 1), :]

    pick_me = (lax.broadcasted_iota(jnp.int32, (GROUP, 128), 0) == me).astype(F32)

    def compute(pair, carry):
        for j in range(2):
            s = 2 * pair + j
            second = chosen_row(s)
            first = 1.0 - second
            for cb in range(D // 128):
                cols = pl.ds(128 * cb, 128)
                for whole, sel in ((tok, xs), (gr, gs)):
                    a = whole[s, pl.ds(0, BLK), cols].astype(F32)
                    b = whole[s, pl.ds(BLK, BLK), cols].astype(F32)
                    sel[s, :, cols] = (a * first + b * second).astype(BF)
        two = pl.ds(2 * pair, 2)
        x = xs[two].reshape(2 * BLK, D)
        wg = wrec[:, pl.ds(0, 32), :].reshape(D, H)
        wu = wrec[:, pl.ds(32, 32), :].reshape(D, H)
        gate_pre = jnp.dot(x, wg, preferred_element_type=F32)
        up_pre = jnp.dot(x, wu, preferred_element_type=F32)
        grad_hidden = None
        for cb in range(4):
            g = gs[two, :, pl.ds(256 * cb, 256)].reshape(2 * BLK, 256)
            w = wd_block(cb)
            term = nt(g, w)
            grad_hidden = term if grad_hidden is None else grad_hidden + term
        weight = jnp.concatenate(
            [
                lax.dot_general(
                    meta[2 * pair + j, pl.ds(0, GROUP), :], pick_me, (((0,), (0,)), ((), ())),
                    preferred_element_type=F32, precision=lax.Precision.HIGHEST,
                )
                for j in range(2)
            ],
            axis=0,
        )
        weight = jnp.concatenate([weight, weight], axis=1)
        sig = 1.0 / (1.0 + jnp.exp(-gate_pre))
        swish = gate_pre * sig
        grad_hidden = grad_hidden * weight
        hact[two] = (swish * up_pre * weight).astype(BF).reshape(2, BLK, H)
        gu = (grad_hidden * swish).astype(BF)
        gg = (grad_hidden * up_pre * sig * (1.0 + gate_pre * (1.0 - sig))).astype(BF)
        gact[two, :, pl.ds(0, H)] = gg.reshape(2, BLK, H)
        gact[two, :, pl.ds(H, H)] = gu.reshape(2, BLK, H)
        back = nt(gg, wg) + nt(gu, wu)
        cbuf[two] = back.astype(BF).reshape(2, BLK, D)
        return carry

    def wd_block(cb):
        rows = pl.ds(64 + 16 * (cb % 2), 16)
        parts = [wrec[2 * i + cb // 2, rows, :] for i in range(16)]
        return jnp.concatenate(parts, axis=0)

    def run(first, last):
        lax.fori_loop(first, last, compute, 0)

    for c in range(3):
        for way in range(2):
            gather(0, way, 1, c).start()
    for c in locals_:
        c.wait()
    each_peer(lambda k: spread(k).start())
    for c in range(3):
        to_mate(c).start()
    mixed[n] = pack[n // 2, lax.rem(n, 2)]
    for c in range(3):
        arrive(0, 1, c)
    for c in range(3):
        arrive(0, 2, c)
    each_peer(lambda k: spread(k).wait_recv())

    def forward(k):
        to = lax.rem(n + k, NODES)
        stage[to] = mixed[partner[to]]
        collect(k).start()

    each_peer(forward)
    wrec[n] = mixed[partner[n]]
    for c in range(3):
        arrive(0, 3, c)
    for c in range(3):
        to_mate(c).wait_recv()
        for way in range(2):
            gather(1, way, 1, c).start()
    for c in range(3):
        arrive(0, 4, c)
    for c in owns:
        c.wait()
    for c in range(3):
        arrive(1, 1, c)
    each_peer(lambda k: collect(k).wait_recv())
    run(0, 1)
    for c in range(2):
        arrive(1, 2, c)
    run(1, 3)
    arrive(1, 2, 2)
    run(3, 6)
    for c in range(3):
        arrive(1, 3, c)
    run(6, 7)
    for c in range(3):
        arrive(1, 4, c)
    run(7, 8)

    outs = [
        pltpu.make_async_copy(dg_v, dg_out, out_sem.at[0]),
        pltpu.make_async_copy(du_v, du_out, out_sem.at[1]),
        pltpu.make_async_copy(dd_v, dd_out, out_sem.at[2]),
        pltpu.make_async_copy(dt_v, dt_out, out_sem.at[3]),
    ]

    def grad_piece(i):
        cols = pl.ds(256 * (i % 4), 256)
        if i < 4:
            x = xs[:, :, cols].reshape(GROUP * BLK, 256)
            both = tn(x, gact[...].reshape(GROUP * BLK, 2 * H))
            dg_v[cols, :] = both[:, :H].astype(BF)
            du_v[cols, :] = both[:, H:].astype(BF)
        else:
            g = gs[:, :, cols].reshape(GROUP * BLK, 256)
            dd_v[:, cols] = tn(hact[...].reshape(GROUP * BLK, H), g).astype(BF)
        if i == 3:
            outs[0].start()
            outs[1].start()
        if i == 7:
            outs[2].start()

    def term(s, c):
        row = chosen_row(s)
        second = jnp.concatenate([row] * (HALF // 128), axis=1)
        mine = cbuf[s, :, pl.ds(HALF * c, HALF)].astype(F32)
        return (mine * (1.0 - second), mine * second)

    def back_copy(q, way, hops, c):
        if hops == 4 or (hops == 3 and c != way):
            src = sbuf.at[q, way, 4 - hops]
        else:
            src = rbuf.at[q, way, hops, c]
        return pltpu.make_async_remote_copy(
            src_ref=src,
            dst_ref=rbuf.at[q, way, hops - 1, c],
            send_sem=rs_send.at[q, way, hops - 1, c],
            recv_sem=rs_recv.at[q, way, hops - 1, c],
            device_id=(n, ring[way]),
            device_id_type=MESH,
        )

    def back_send(q, way, hops, c):
        parts = term(q * 8 + slot(hops, 1 - way), c)
        if hops == 4 or (hops == 3 and c != way):
            for b in range(2):
                sbuf[q, way, 4 - hops, b] = parts[b].astype(BF)
        else:
            back_copy(q, way, hops + 1, c).wait_recv()
            for b in range(2):
                rbuf[q, way, hops, c, b] = (
                    rbuf[q, way, hops, c, b].astype(F32) + parts[b]
                ).astype(BF)
        back_copy(q, way, hops, c).start()

    steps = [
        (q, hops, turn)
        for q in (1, 0)
        for hops in (4, 3, 2, 1)
        for turn in range(2)
        if hops < 4 or turn == 0
    ]

    def z_copy(c):
        return pltpu.make_async_remote_copy(
            src_ref=zsend.at[c],
            dst_ref=zrecv.at[c],
            send_sem=z_send.at[c],
            recv_sem=z_recv.at[c],
            device_id=(n, mate),
            device_id_type=MESH,
        )

    def total(q, c):
        parts = term(q * 8, c)
        for way in range(2):
            back_copy(q, way, 1, c).wait_recv()
        return [
            parts[b] + rbuf[q, 0, 0, c, b].astype(F32) + rbuf[q, 1, 0, c, b].astype(F32)
            for b in range(2)
        ]

    for i, (q, hops, turn) in enumerate(steps):
        for way in range(2):
            back_send(q, way, hops, way ^ turn)
        if i < 8:
            grad_piece(i)
        if i == 7:
            for c in range(2):
                sums = total(1, c)
                for b in range(2):
                    zsend[c, b] = sums[b].astype(BF)
                z_copy(c).start()
    for c in range(2):
        sums = total(0, c)
        z_copy(c).wait_recv()
        for b in range(2):
            dt_v[pl.ds(BLK * b, BLK), pl.ds(HALF * c, HALF)] = (
                sums[b] + zrecv[c, b].astype(F32)
            ).astype(BF)
    outs[3].start()

    for q in range(2):
        for hops in range(1, 5):
            for c in range(3):
                for way in range(2):
                    if has(way, hops, c):
                        gather(q, way, hops, c).wait_send()
    for c in range(3):
        to_mate(c).wait_send()
    each_peer(lambda k: spread(k).wait_send())
    each_peer(lambda k: collect(k).wait_send())
    for q, hops, turn in steps:
        for way in range(2):
            back_copy(q, way, hops, way ^ turn).wait_send()
    for c in range(2):
        z_copy(c).wait_send()
    for c in outs:
        c.wait()


def on_device(tokens, grad_out, router_gate, counts, routes, partner, w_gate, w_up, w_down):
    groups = jnp.arange(GROUP, dtype=jnp.int32)
    live = jnp.arange(2, dtype=jnp.int32) < counts[0]
    gates = router_gate.T.reshape(4, 2, 1, BLK)
    hot = (routes[0].T[:, :, None] == groups) & live[None, :, None]
    weights = jnp.sum(jnp.where(hot[:, :, :, None], gates, 0.0), axis=(0, 1))
    second = jnp.any(routes[0, 1][:, None] == groups, axis=0).astype(F32)
    meta = jnp.concatenate([weights, jnp.broadcast_to(second[:, None], (GROUP, BLK))], axis=0)

    any_ = pl.BlockSpec(memory_space=pl.ANY)
    dma = pltpu.SemaphoreType.DMA
    shape = jax.ShapeDtypeStruct
    outs = pl.pallas_call(
        kernel,
        out_shape=(
            shape((2 * BLK, D), BF), shape((D, H), BF), shape((D, H), BF), shape((H, D), BF),
        ),
        in_specs=[pl.BlockSpec(memory_space=pltpu.SMEM)] + [any_] * 6,
        out_specs=[any_] * 4,
        scratch_shapes=[
            pltpu.VMEM((16, 32, 128), F32),
            pltpu.VMEM((16, 2 * BLK, D), BF),
            pltpu.VMEM((16, 2 * BLK, D), BF),
            pltpu.VMEM((16, BLK, D), BF),
            pltpu.VMEM((16, BLK, D), BF),
            pltpu.VMEM((16, BLK, 2 * H), BF),
            pltpu.VMEM((16, BLK, H), BF),
            pltpu.VMEM((16, BLK, D), BF),
            pltpu.VMEM((2, 2, 4, 2, 2, BLK, HALF), BF),
            pltpu.VMEM((2, 2, 2, 2, BLK, HALF), BF),
            pltpu.VMEM((2, 2, BLK, HALF), BF),
            pltpu.VMEM((2, 2, BLK, HALF), BF),
            pltpu.VMEM((16, 2, PART, H), BF),
            pltpu.VMEM((NODES, PART, H), BF),
            pltpu.VMEM((NODES, PART, H), BF),
            pltpu.VMEM((NODES, PART, H), BF),
            pltpu.VMEM((D, H), BF),
            pltpu.VMEM((D, H), BF),
            pltpu.VMEM((H, D), BF),
            pltpu.VMEM((2 * BLK, D), BF),
            dma((2, 2, 4, 3)), dma((2, 2, 4, 3)), dma((3,)), dma((3,)),
            dma((NODES,)), dma((NODES,)), dma((NODES,)), dma((NODES,)),
            dma((2, 2, 4, 2)), dma((2, 2, 4, 2)), dma((2,)), dma((2,)), dma((9,)), dma((4,)),
        ],
        compiler_params=pltpu.CompilerParams(
            collective_id=0, has_side_effects=True, vmem_limit_bytes=67043328
        ),
        name="moe_step",
    )(
        partner, meta, tokens, grad_out,
        w_gate.reshape(16, 2, 32, H), w_up.reshape(16, 2, 32, H), w_down.reshape(16, 16, D),
    )
    dt, dg, du, dd = outs
    return dt, dg.reshape(1, D, H), du.reshape(1, D, H), dd.reshape(1, H, D)


def solution(mesh):
    rows = P(("node", "group"), None)
    cube = P(("node", "group"), None, None)
    return jax.shard_map(
        on_device,
        mesh=mesh,
        in_specs=(rows, rows, rows, P(("node", "group")), cube, P(), cube, cube, cube),
        out_specs=(rows, cube, cube, cube),
        check_vma=False,
    )
```

```python
import functools

import jax
import jax.numpy as jnp
from jax import lax
from jax.experimental import pallas as pl
from jax.experimental.pallas import tpu as pltpu
from jax.sharding import PartitionSpec as P

BF = jnp.bfloat16
F32 = jnp.float32
MESH = pl.DeviceIdType.MESH
NODES = 32
GROUP = 16
RING = 8
BLK = 128
D = 1024
H = 256
HALF = D // 2
PART = 96


def slot(hops, way):
    if hops == 0:
        return 0
    return 7 if hops == RING // 2 else 2 * hops - 1 + way


def nt(left, right):
    return lax.dot_general(left, right, (((1,), (1,)), ((), ())), preferred_element_type=F32)


def tn(left, right):
    return lax.dot_general(left, right, (((0,), (0,)), ((), ())), preferred_element_type=F32)


def kernel(
    partner, meta_in, tok_in, gr_in, wg_in, wu_in, wd_in,
    dt_out, dg_out, du_out, dd_out,
    meta, tok, gr, xs, gs, gact, hact, cbuf, cut, relay, zrel, raw, near, far, sbuf, rbuf, zsend, zrecv, zmeta,
    pack, mixed, stage, wrec, dg_v, du_v, dd_v, dt_v,
    g_send, g_recv, s_send, s_recv, m_send, m_recv, wa_send, wa_recv, wb_send, wb_recv,
    r_send, r_recv, rs_send, rs_recv, z_send, z_recv, loc, out_sem,
):
    n = lax.axis_index("node")
    me = lax.axis_index("group")
    y = me // 2
    side = me % 2
    ring = (lax.rem(y + 1, RING) * 2 + side, lax.rem(y + RING - 1, RING) * 2 + side)
    mate = y * 2 + (1 - side)
    turned = (n >= NODES // 2).astype(jnp.int32)
    zside = (y * 2 + lax.rem(side + turned, 2), y * 2 + lax.rem(side + 1 - turned, 2))
    beyond = (lax.rem(y + 2, RING) * 2 + side, lax.rem(y + RING - 2, RING) * 2 + side)

    locals_ = [
        pltpu.make_async_copy(wg_in, pack.at[:, :, pl.ds(0, 32), :], loc.at[0]),
        pltpu.make_async_copy(wu_in, pack.at[:, :, pl.ds(32, 32), :], loc.at[1]),
    ]
    for cb in range(4):
        locals_.append(
            pltpu.make_async_copy(
                wd_in.at[:, :, pl.ds(256 * cb, 256)],
                pack.at[:, cb // 2, pl.ds(64 + 16 * (cb % 2), 16), :],
                loc.at[2 + cb],
            )
        )
    owns = [
        pltpu.make_async_copy(meta_in, meta.at[0, 0], loc.at[6]),
        pltpu.make_async_copy(tok_in, tok.at[0, 0], loc.at[7]),
        pltpu.make_async_copy(gr_in, gr.at[0, 0], loc.at[8]),
    ]
    for c in locals_ + owns:
        c.start()

    barrier = pltpu.get_barrier_semaphore()

    def greet(k, carry):
        pl.semaphore_signal(
            barrier, inc=1, device_id=(lax.rem(n + k, NODES), me), device_id_type=MESH
        )
        return carry

    for g in (ring[0], ring[1], mate):
        pl.semaphore_signal(barrier, inc=1, device_id=(n, g), device_id_type=MESH)
    lax.fori_loop(1, NODES, greet, 0)
    pl.semaphore_signal(
        barrier, inc=1, device_id=(lax.rem(n + NODES // 2, NODES), mate), device_id_type=MESH
    )
    pl.semaphore_wait(barrier, NODES - 1 + 4)

    bufs = (meta, tok, gr)
    ins = (meta_in, tok_in, gr_in)

    def gather(q, way, hops, c):
        src = ins[c] if q == 0 and hops == 1 else bufs[c].at[q, slot(hops - 1, way)]
        return pltpu.make_async_remote_copy(
            src_ref=src,
            dst_ref=bufs[c].at[q, slot(hops, way)],
            send_sem=g_send.at[q, way, hops - 1, c],
            recv_sem=g_recv.at[q, way, hops - 1, c],
            device_id=(n, ring[way]),
            device_id_type=MESH,
        )

    def cut_copy(q, way, k):
        if k < 2:
            dst = (xs, gs)[k].at[q * 8 + slot(3, way)]
        else:
            dst = relay.at[q, way]
        return pltpu.make_async_remote_copy(
            src_ref=cut.at[q, way, k],
            dst_ref=dst,
            send_sem=s_send.at[q, way, k],
            recv_sem=s_recv.at[q, way, k],
            device_id=(n, ring[way]),
            device_id_type=MESH,
        )

    def last_copy(q, way):
        return pltpu.make_async_remote_copy(
            src_ref=relay.at[q, way],
            dst_ref=(xs, gs)[way].at[q * 8 + 7],
            send_sem=s_send.at[q, way, 3],
            recv_sem=s_recv.at[q, way, 3],
            device_id=(n, ring[way]),
            device_id_type=MESH,
        )

    def to_mate(c, leg):
        stop = zrel.at[c - 1] if c else zmeta
        return pltpu.make_async_remote_copy(
            src_ref=ins[c] if leg == 0 else stop,
            dst_ref=stop if leg == 0 else bufs[c].at[1, 0],
            send_sem=m_send.at[c, leg],
            recv_sem=m_recv.at[c, leg],
            device_id=(lax.rem(n + NODES // 2, NODES), zside[1 if c == 2 else 0]),
            device_id_type=MESH,
        )

    def spread(k):
        to = lax.rem(n + k, NODES)
        return pltpu.make_async_remote_copy(
            src_ref=pack.at[to // 2, lax.rem(to, 2)],
            dst_ref=mixed.at[n],
            send_sem=wa_send.at[k],
            recv_sem=wa_recv.at[k],
            device_id=(to, me),
            device_id_type=MESH,
        )

    def collect(k):
        to = lax.rem(n + k, NODES)
        return pltpu.make_async_remote_copy(
            src_ref=stage.at[to],
            dst_ref=wrec.at[n],
            send_sem=wb_send.at[k],
            recv_sem=wb_recv.at[k],
            device_id=(to, me),
            device_id_type=MESH,
        )

    def each_peer(act):
        def body(k, carry):
            act(k)
            return carry

        lax.fori_loop(1, NODES, body, 0)

    def row_of(q, r, who):
        return meta[q, r, pl.ds(GROUP + who, 1), :]

    def choose(q, r, c, who, dst):
        second = row_of(q, r, who)
        first = 1.0 - second
        for cb in range(D // 128):
            cols = pl.ds(128 * cb, 128)
            a = bufs[c][q, r, pl.ds(0, BLK), cols].astype(F32)
            b = bufs[c][q, r, pl.ds(BLK, BLK), cols].astype(F32)
            dst[:, cols] = (a * first + b * second).astype(BF)

    def arrive(q, hops, c):
        if hops == 1:
            for way in range(2):
                gather(q, way, 1, c).wait_recv()
                gather(q, way, 2, c).start()
        elif hops == 2:
            for way in range(2):
                gather(q, way, 2, c).wait_recv()
                if c == 0:
                    gather(q, way, 3, 0).start()
                    continue
                if c == 1 + way:
                    choose(q, slot(2, way), c, beyond[way], cut.at[q, way, 2])
                    cut_copy(q, way, 2).start()
                choose(q, slot(2, way), c, ring[way], cut.at[q, way, c - 1])
                cut_copy(q, way, c - 1).start()
        elif hops == 3:
            for way in range(2):
                if c == 0:
                    gather(q, way, 3, 0).wait_recv()
                    if way == 0:
                        gather(q, way, 4, 0).start()
                    continue
                if c == 1 + way:
                    cut_copy(q, way, 2).wait_recv()
                    last_copy(q, way).start()
                cut_copy(q, way, c - 1).wait_recv()
        elif c == 0:
            gather(q, 0, 4, 0).wait_recv()
        else:
            last_copy(q, c - 1).wait_recv()

    pick_me = (lax.broadcasted_iota(jnp.int32, (GROUP, 128), 0) == me).astype(F32)

    def compute(pair, carry):
        two = pl.ds(2 * pair, 2)
        x = xs[two].reshape(2 * BLK, D)
        wg = wrec[:, pl.ds(0, 32), :].reshape(D, H)
        wu = wrec[:, pl.ds(32, 32), :].reshape(D, H)
        gate_pre = jnp.dot(x, wg, preferred_element_type=F32)
        up_pre = jnp.dot(x, wu, preferred_element_type=F32)
        grad_hidden = None
        for cb in range(4):
            g = gs[two, :, pl.ds(256 * cb, 256)].reshape(2 * BLK, 256)
            w = wd_block(cb)
            term = nt(g, w)
            grad_hidden = term if grad_hidden is None else grad_hidden + term
        weight = jnp.concatenate(
            [
                lax.dot_general(
                    meta[pair // 4, 2 * lax.rem(pair, 4) + j, pl.ds(0, GROUP), :], pick_me, (((0,), (0,)), ((), ())),
                    preferred_element_type=F32, precision=lax.Precision.HIGHEST,
                )
                for j in range(2)
            ],
            axis=0,
        )
        weight = jnp.concatenate([weight, weight], axis=1)
        sig = 1.0 / (1.0 + jnp.exp(-gate_pre))
        swish = gate_pre * sig
        grad_hidden = grad_hidden * weight
        hact[two] = (swish * up_pre * weight).astype(BF).reshape(2, BLK, H)
        gu = (grad_hidden * swish).astype(BF)
        gg = (grad_hidden * up_pre * sig * (1.0 + gate_pre * (1.0 - sig))).astype(BF)
        gact[two, :, pl.ds(0, H)] = gg.reshape(2, BLK, H)
        gact[two, :, pl.ds(H, H)] = gu.reshape(2, BLK, H)
        back = nt(gg, wg) + nt(gu, wu)
        cbuf[two] = back.astype(BF).reshape(2, BLK, D)
        return carry

    def wd_block(cb):
        rows = pl.ds(64 + 16 * (cb % 2), 16)
        parts = [wrec[2 * i + cb // 2, rows, :] for i in range(16)]
        return jnp.concatenate(parts, axis=0)

    def run(first, last):
        lax.fori_loop(first, last, compute, 0)

    def pick(q, first, last):
        def body(r, carry):
            for c, sel in ((1, xs), (2, gs)):
                choose(q, r, c, me, sel.at[q * 8 + r])
            return carry

        lax.fori_loop(first, last, body, 0)

    def raw_copy(q, way, k):
        if k == 2:
            src, dst = cbuf.at[q * 8 + 7, :, pl.ds(HALF * way, HALF)], near.at[q, way]
        elif k == 3:
            src, dst = near.at[q, way], far.at[q, way]
        else:
            src = cbuf.at[q * 8 + slot(3, 1 - way), :, pl.ds(HALF * k, HALF)]
            dst = raw.at[q, way, k]
        return pltpu.make_async_remote_copy(
            src_ref=src,
            dst_ref=dst,
            send_sem=r_send.at[q, way, k],
            recv_sem=r_recv.at[q, way, k],
            device_id=(n, ring[way]),
            device_id_type=MESH,
        )

    for c in range(3):
        for way in range(2):
            gather(0, way, 1, c).start()
    for c in range(3):
        to_mate(c, 0).start()
    for c in locals_:
        c.wait()
    mixed[n] = pack[n // 2, lax.rem(n, 2)]
    for c in owns:
        c.wait()
    pick(0, 0, 1)
    for c in range(2):
        arrive(0, 1, c)
    for c in range(2):
        to_mate(c, 0).wait_recv()
        to_mate(c, 1).start()
    arrive(0, 1, 2)
    to_mate(2, 0).wait_recv()
    to_mate(2, 1).start()
    each_peer(lambda k: spread(k).start())
    pick(0, 1, 3)
    for c in range(3):
        arrive(0, 2, c)
    pick(0, 3, 5)
    for c in range(2):
        arrive(0, 3, c)
    for c in range(2):
        to_mate(c, 1).wait_recv()
        for way in range(2):
            gather(1, way, 1, c).start()
    arrive(0, 3, 2)
    to_mate(2, 1).wait_recv()
    for way in range(2):
        gather(1, way, 1, 2).start()
    pick(1, 0, 1)
    for c in range(3):
        arrive(0, 4, c)
    each_peer(lambda k: spread(k).wait_recv())

    def forward(k):
        to = lax.rem(n + k, NODES)
        stage[to] = mixed[partner[to]]
        collect(k).start()

    each_peer(forward)
    wrec[n] = mixed[partner[n]]
    for c in range(3):
        arrive(1, 1, c)
    pick(1, 1, 3)
    for c in range(3):
        arrive(1, 2, c)
    pick(1, 3, 5)
    each_peer(lambda k: collect(k).wait_recv())
    run(0, 2)
    for c in range(2):
        arrive(1, 3, c)
    run(2, 4)
    arrive(1, 3, 2)
    for way in range(2):
        for k in (2, 0, 1):
            raw_copy(0, way, k).start()
    run(4, 7)
    for c in range(3):
        arrive(1, 4, c)
    run(7, 8)

    outs = [
        pltpu.make_async_copy(dg_v, dg_out, out_sem.at[0]),
        pltpu.make_async_copy(du_v, du_out, out_sem.at[1]),
        pltpu.make_async_copy(dd_v, dd_out, out_sem.at[2]),
        pltpu.make_async_copy(dt_v, dt_out, out_sem.at[3]),
    ]

    def grad_piece(i):
        cols = pl.ds(256 * (i % 4), 256)
        if i < 4:
            x = xs[:, :, cols].reshape(GROUP * BLK, 256)
            both = tn(x, gact[...].reshape(GROUP * BLK, 2 * H))
            dg_v[cols, :] = both[:, :H].astype(BF)
            du_v[cols, :] = both[:, H:].astype(BF)
        else:
            g = gs[:, :, cols].reshape(GROUP * BLK, 256)
            dd_v[:, cols] = tn(hact[...].reshape(GROUP * BLK, H), g).astype(BF)
        if i == 3:
            outs[0].start()
            outs[1].start()
        if i == 7:
            outs[2].start()

    def wide(row):
        return jnp.concatenate([row] * (HALF // 128), axis=1)

    def placed(block, row):
        second = wide(row)
        block = block.astype(F32)
        return (block * (1.0 - second), block * second)

    def term(q, r, c):
        return placed(cbuf[q * 8 + r, :, pl.ds(HALF * c, HALF)], row_of(q, r, me))

    def back_copy(q, way, hops, c):
        return pltpu.make_async_remote_copy(
            src_ref=sbuf.at[q, way, c] if hops == 2 else rbuf.at[q, way, 1, c],
            dst_ref=rbuf.at[q, way, hops - 1, c],
            send_sem=rs_send.at[q, way, hops - 1, c],
            recv_sem=rs_recv.at[q, way, hops - 1, c],
            device_id=(n, ring[way]),
            device_id_type=MESH,
        )

    def back_send(q, way, hops, c):
        r = slot(hops, 1 - way)
        if hops == 4:
            if q == 1:
                raw_copy(q, way, 2).start()
            return
        if hops == 3:
            if c == way:
                raw_copy(q, way, 2).wait_recv()
                raw_copy(q, way, 3).start()
            if q == 1:
                raw_copy(q, way, c).start()
            return
        sums = term(q, r, c)
        if hops == 2:
            raw_copy(q, way, c).wait_recv()
            more = placed(raw[q, way, c], row_of(q, r, ring[1 - way]))
            sums = [u + v for u, v in zip(sums, more)]
            if c == way:
                raw_copy(q, way, 3).wait_recv()
                more = placed(far[q, way], row_of(q, r, beyond[1 - way]))
                sums = [u + v for u, v in zip(sums, more)]
            for b in range(2):
                sbuf[q, way, c, b] = sums[b].astype(BF)
        else:
            back_copy(q, way, 2, c).wait_recv()
            for b in range(2):
                rbuf[q, way, 1, c, b] = (rbuf[q, way, 1, c, b].astype(F32) + sums[b]).astype(BF)
        back_copy(q, way, hops, c).start()

    steps = [
        (q, hops, turn)
        for q in (1, 0)
        for hops in (4, 3, 2, 1)
        for turn in range(2)
        if hops < 4 or turn == 0
    ]

    def z_copy(c):
        return pltpu.make_async_remote_copy(
            src_ref=zsend.at[c],
            dst_ref=zrecv.at[c],
            send_sem=z_send.at[c],
            recv_sem=z_recv.at[c],
            device_id=(n, mate),
            device_id_type=MESH,
        )

    def total(q, c):
        parts = term(q, 0, c)
        for way in range(2):
            back_copy(q, way, 1, c).wait_recv()
        return [
            parts[b] + rbuf[q, 0, 0, c, b].astype(F32) + rbuf[q, 1, 0, c, b].astype(F32)
            for b in range(2)
        ]

    for i, (q, hops, turn) in enumerate(steps):
        for way in range(2):
            back_send(q, way, hops, way ^ turn)
        if i < 8:
            grad_piece(i)
        if i == 7:
            for c in range(2):
                sums = total(1, c)
                for b in range(2):
                    zsend[c, b] = sums[b].astype(BF)
                z_copy(c).start()
    for c in range(2):
        sums = total(0, c)
        z_copy(c).wait_recv()
        for b in range(2):
            dt_v[pl.ds(BLK * b, BLK), pl.ds(HALF * c, HALF)] = (
                sums[b] + zrecv[c, b].astype(F32)
            ).astype(BF)
    outs[3].start()

    for q in range(2):
        for way in range(2):
            for c in range(3):
                gather(q, way, 1, c).wait_send()
                gather(q, way, 2, c).wait_send()
                cut_copy(q, way, c).wait_send()
            gather(q, way, 3, 0).wait_send()
            if way == 0:
                gather(q, way, 4, 0).wait_send()
            last_copy(q, way).wait_send()
            for k in range(4):
                raw_copy(q, way, k).wait_send()
            for hops in (2, 1):
                for c in range(2):
                    back_copy(q, way, hops, c).wait_send()
    for c in range(3):
        for leg in range(2):
            to_mate(c, leg).wait_send()
    each_peer(lambda k: spread(k).wait_send())
    each_peer(lambda k: collect(k).wait_send())
    for c in range(2):
        z_copy(c).wait_send()
    for c in outs:
        c.wait()


def on_device(tokens, grad_out, router_gate, counts, routes, partner, w_gate, w_up, w_down):
    groups = jnp.arange(GROUP, dtype=jnp.int32)
    live = jnp.arange(2, dtype=jnp.int32) < counts[0]
    gates = router_gate.T.reshape(4, 2, 1, BLK)
    hot = (routes[0].T[:, :, None] == groups) & live[None, :, None]
    weights = jnp.sum(jnp.where(hot[:, :, :, None], gates, 0.0), axis=(0, 1))
    second = jnp.any(routes[0, 1][:, None] == groups, axis=0).astype(F32)
    meta = jnp.concatenate([weights, jnp.broadcast_to(second[:, None], (GROUP, BLK))], axis=0)

    any_ = pl.BlockSpec(memory_space=pl.ANY)
    dma = pltpu.SemaphoreType.DMA
    shape = jax.ShapeDtypeStruct
    outs = pl.pallas_call(
        kernel,
        out_shape=(
            shape((2 * BLK, D), BF), shape((D, H), BF), shape((D, H), BF), shape((H, D), BF),
        ),
        in_specs=[pl.BlockSpec(memory_space=pltpu.SMEM)] + [any_] * 6,
        out_specs=[any_] * 4,
        scratch_shapes=[
            pltpu.VMEM((2, 8, 32, 128), F32),
            pltpu.VMEM((2, 5, 2 * BLK, D), BF),
            pltpu.VMEM((2, 5, 2 * BLK, D), BF),
            pltpu.VMEM((16, BLK, D), BF),
            pltpu.VMEM((16, BLK, D), BF),
            pltpu.VMEM((16, BLK, 2 * H), BF),
            pltpu.VMEM((16, BLK, H), BF),
            pltpu.VMEM((16, BLK, D), BF),
            pltpu.VMEM((2, 2, 3, BLK, D), BF),
            pltpu.VMEM((2, 2, BLK, D), BF),
            pltpu.VMEM((2, 2 * BLK, D), BF),
            pltpu.VMEM((2, 2, 2, BLK, HALF), BF),
            pltpu.VMEM((2, 2, BLK, HALF), BF),
            pltpu.VMEM((2, 2, BLK, HALF), BF),
            pltpu.VMEM((2, 2, 2, 2, BLK, HALF), BF),
            pltpu.VMEM((2, 2, 2, 2, 2, BLK, HALF), BF),
            pltpu.VMEM((2, 2, BLK, HALF), BF),
            pltpu.VMEM((2, 2, BLK, HALF), BF),
            pltpu.VMEM((32, 128), F32),
            pltpu.VMEM((16, 2, PART, H), BF),
            pltpu.VMEM((NODES, PART, H), BF),
            pltpu.VMEM((NODES, PART, H), BF),
            pltpu.VMEM((NODES, PART, H), BF),
            pltpu.VMEM((D, H), BF),
            pltpu.VMEM((D, H), BF),
            pltpu.VMEM((H, D), BF),
            pltpu.VMEM((2 * BLK, D), BF),
            dma((2, 2, 4, 3)), dma((2, 2, 4, 3)), dma((2, 2, 4)), dma((2, 2, 4)), dma((3, 2)), dma((3, 2)),
            dma((NODES,)), dma((NODES,)), dma((NODES,)), dma((NODES,)),
            dma((2, 2, 4)), dma((2, 2, 4)), dma((2, 2, 2, 2)), dma((2, 2, 2, 2)), dma((2,)), dma((2,)), dma((9,)), dma((4,)),
        ],
        compiler_params=pltpu.CompilerParams(
            collective_id=0, has_side_effects=True, vmem_limit_bytes=67043328
        ),
        name="moe_step",
    )(
        partner, meta, tokens, grad_out,
        w_gate.reshape(16, 2, 32, H), w_up.reshape(16, 2, 32, H), w_down.reshape(16, 16, D),
    )
    dt, dg, du, dd = outs
    return dt, dg.reshape(1, D, H), du.reshape(1, D, H), dd.reshape(1, H, D)


def solution(mesh):
    rows = P(("node", "group"), None)
    cube = P(("node", "group"), None, None)
    return jax.shard_map(
        on_device,
        mesh=mesh,
        in_specs=(rows, rows, rows, P(("node", "group")), cube, P(), cube, cube, cube),
        out_specs=(rows, cube, cube, cube),
        check_vma=False,
    )
```

```python
import functools

import jax
import jax.numpy as jnp
from jax import lax
from jax.experimental import pallas as pl
from jax.experimental.pallas import tpu as pltpu
from jax.sharding import PartitionSpec as P

BF = jnp.bfloat16
F32 = jnp.float32
MESH = pl.DeviceIdType.MESH
NODES = 32
GROUP = 16
RING = 8
BLK = 128
D = 1024
H = 256
XW = 640
XC = ((0, 384), (384, 256))
ZC = ((640, 256), (896, 128))
PART = 96


def slot(hops, way):
    if hops == 0:
        return 0
    return 7 if hops == RING // 2 else 2 * hops - 1 + way


def nt(left, right):
    return lax.dot_general(left, right, (((1,), (1,)), ((), ())), preferred_element_type=F32)


def tn(left, right):
    return lax.dot_general(left, right, (((0,), (0,)), ((), ())), preferred_element_type=F32)


def kernel(
    partner, meta_in, tok_in, gr_in, wg_in, wu_in, wd_in,
    dt_out, dg_out, du_out, dd_out,
    meta, tok, gr, xs, gs, gact, hact, cbuf, cut, relay, zrel, zmeta,
    raw, near, far, sbuf, rbuf, zst, zr, zf, cm, zsend, zl, zrecv,
    pack, mixed, stage, wrec, dg_v, du_v, dd_v, dt_v,
    g_send, g_recv, s_send, s_recv, m_send, m_recv, wa_send, wa_recv, wb_send, wb_recv,
    r_send, r_recv, rs_send, rs_recv, t_send, t_recv, f_send, f_recv, z_send, z_recv, loc, out_sem,
):
    n = lax.axis_index("node")
    me = lax.axis_index("group")
    y = me // 2
    side = me % 2
    ring = (lax.rem(y + 1, RING) * 2 + side, lax.rem(y + RING - 1, RING) * 2 + side)
    mate = y * 2 + (1 - side)
    turned = (n >= NODES // 2).astype(jnp.int32)
    zside = (y * 2 + lax.rem(side + turned, 2), y * 2 + lax.rem(side + 1 - turned, 2))
    beyond = (lax.rem(y + 2, RING) * 2 + side, lax.rem(y + RING - 2, RING) * 2 + side)

    locals_ = [
        pltpu.make_async_copy(wg_in, pack.at[:, :, pl.ds(0, 32), :], loc.at[0]),
        pltpu.make_async_copy(wu_in, pack.at[:, :, pl.ds(32, 32), :], loc.at[1]),
    ]
    for cb in range(4):
        locals_.append(
            pltpu.make_async_copy(
                wd_in.at[:, :, pl.ds(256 * cb, 256)],
                pack.at[:, cb // 2, pl.ds(64 + 16 * (cb % 2), 16), :],
                loc.at[2 + cb],
            )
        )
    owns = [
        pltpu.make_async_copy(meta_in, meta.at[0, 0], loc.at[6]),
        pltpu.make_async_copy(tok_in, tok.at[0, 0], loc.at[7]),
        pltpu.make_async_copy(gr_in, gr.at[0, 0], loc.at[8]),
    ]
    for c in locals_ + owns:
        c.start()

    barrier = pltpu.get_barrier_semaphore()

    def greet(k, carry):
        pl.semaphore_signal(
            barrier, inc=1, device_id=(lax.rem(n + k, NODES), me), device_id_type=MESH
        )
        return carry

    for g in ring:
        pl.semaphore_signal(barrier, inc=1, device_id=(n, g), device_id_type=MESH)
    lax.fori_loop(1, NODES, greet, 0)
    pl.semaphore_signal(
        barrier, inc=1, device_id=(lax.rem(n + NODES // 2, NODES), mate), device_id_type=MESH
    )
    pl.semaphore_wait(barrier, NODES - 1 + 3)

    bufs = (meta, tok, gr)
    ins = (meta_in, tok_in, gr_in)

    def gather(q, way, hops, c):
        src = ins[c] if q == 0 and hops == 1 else bufs[c].at[q, slot(hops - 1, way)]
        return pltpu.make_async_remote_copy(
            src_ref=src,
            dst_ref=bufs[c].at[q, slot(hops, way)],
            send_sem=g_send.at[q, way, hops - 1, c],
            recv_sem=g_recv.at[q, way, hops - 1, c],
            device_id=(n, ring[way]),
            device_id_type=MESH,
        )

    def cut_copy(q, way, k):
        if k < 2:
            dst = (xs, gs)[k].at[q * 8 + slot(3, way)]
        else:
            dst = relay.at[q, way]
        return pltpu.make_async_remote_copy(
            src_ref=cut.at[q, way, k],
            dst_ref=dst,
            send_sem=s_send.at[q, way, k],
            recv_sem=s_recv.at[q, way, k],
            device_id=(n, ring[way]),
            device_id_type=MESH,
        )

    def last_copy(q, way):
        return pltpu.make_async_remote_copy(
            src_ref=relay.at[q, way],
            dst_ref=(xs, gs)[way].at[q * 8 + 7],
            send_sem=s_send.at[q, way, 3],
            recv_sem=s_recv.at[q, way, 3],
            device_id=(n, ring[way]),
            device_id_type=MESH,
        )

    def to_mate(c, leg):
        stop = zrel.at[c - 1] if c else zmeta
        return pltpu.make_async_remote_copy(
            src_ref=ins[c] if leg == 0 else stop,
            dst_ref=stop if leg == 0 else bufs[c].at[1, 0],
            send_sem=m_send.at[c, leg],
            recv_sem=m_recv.at[c, leg],
            device_id=(lax.rem(n + NODES // 2, NODES), zside[1 if c == 2 else 0]),
            device_id_type=MESH,
        )

    def flip(k):
        return sum(lax.rem(n // (1 << i) + k // (1 << i), 2) * (1 << i) for i in range(5))

    def spread(k):
        to = flip(k)
        return pltpu.make_async_remote_copy(
            src_ref=pack.at[to // 2, lax.rem(to, 2)],
            dst_ref=mixed.at[n],
            send_sem=wa_send.at[k],
            recv_sem=wa_recv.at[k],
            device_id=(to, me),
            device_id_type=MESH,
        )

    def collect(k):
        to = flip(k)
        return pltpu.make_async_remote_copy(
            src_ref=stage.at[to],
            dst_ref=wrec.at[n],
            send_sem=wb_send.at[k],
            recv_sem=wb_recv.at[k],
            device_id=(to, me),
            device_id_type=MESH,
        )

    def each_peer(act):
        def body(k, carry):
            act(k)
            return carry

        lax.fori_loop(1, NODES, body, 0)

    def row_of(q, r, who):
        return (meta[q, r, pl.ds(who, 1), :] < 0.0).astype(F32)

    def choose(q, r, c, who, dst):
        second = row_of(q, r, who)
        first = 1.0 - second
        for cb in range(D // 128):
            cols = pl.ds(128 * cb, 128)
            a = bufs[c][q, r, pl.ds(0, BLK), cols].astype(F32)
            b = bufs[c][q, r, pl.ds(BLK, BLK), cols].astype(F32)
            dst[:, cols] = (a * first + b * second).astype(BF)

    def arrive(q, hops, c):
        if hops == 1:
            for way in range(2):
                gather(q, way, 1, c).wait_recv()
                gather(q, way, 2, c).start()
        elif hops == 2:
            for way in range(2):
                gather(q, way, 2, c).wait_recv()
                if c == 0:
                    gather(q, way, 3, 0).start()
                    continue
                if c == 1 + way:
                    choose(q, slot(2, way), c, beyond[way], cut.at[q, way, 2])
                    cut_copy(q, way, 2).start()
                choose(q, slot(2, way), c, ring[way], cut.at[q, way, c - 1])
                cut_copy(q, way, c - 1).start()
        elif hops == 3:
            for way in range(2):
                if c == 0:
                    gather(q, way, 3, 0).wait_recv()
                    if way == 0:
                        gather(q, way, 4, 0).start()
                    continue
                if c == 1 + way:
                    cut_copy(q, way, 2).wait_recv()
                    last_copy(q, way).start()
                cut_copy(q, way, c - 1).wait_recv()
        elif c == 0:
            gather(q, 0, 4, 0).wait_recv()
        else:
            last_copy(q, c - 1).wait_recv()

    pick_me = (lax.broadcasted_iota(jnp.int32, (GROUP, 128), 0) == me).astype(F32)

    def compute(pair, carry):
        two = pl.ds(2 * pair, 2)
        x = xs[two].reshape(2 * BLK, D)
        wg = wrec[:, pl.ds(0, 32), :].reshape(D, H)
        wu = wrec[:, pl.ds(32, 32), :].reshape(D, H)
        gate_pre = jnp.dot(x, wg, preferred_element_type=F32)
        up_pre = jnp.dot(x, wu, preferred_element_type=F32)
        grad_hidden = None
        for cb in range(4):
            g = gs[two, :, pl.ds(256 * cb, 256)].reshape(2 * BLK, 256)
            w = wd_block(cb)
            term = nt(g, w)
            grad_hidden = term if grad_hidden is None else grad_hidden + term
        weight = jnp.concatenate(
            [
                lax.dot_general(
                    meta[pair // 4, 2 * lax.rem(pair, 4) + j], pick_me, (((0,), (0,)), ((), ())),
                    preferred_element_type=F32, precision=lax.Precision.HIGHEST,
                )
                for j in range(2)
            ],
            axis=0,
        )
        weight = jnp.abs(jnp.concatenate([weight, weight], axis=1))
        sig = 1.0 / (1.0 + jnp.exp(-gate_pre))
        swish = gate_pre * sig
        grad_hidden = grad_hidden * weight
        hact[two] = (swish * up_pre * weight).astype(BF).reshape(2, BLK, H)
        gu = (grad_hidden * swish).astype(BF)
        gg = (grad_hidden * up_pre * sig * (1.0 + gate_pre * (1.0 - sig))).astype(BF)
        gact[two, :, pl.ds(0, H)] = gg.reshape(2, BLK, H)
        gact[two, :, pl.ds(H, H)] = gu.reshape(2, BLK, H)
        back = nt(gg, wg) + nt(gu, wu)
        cbuf[two] = back.astype(BF).reshape(2, BLK, D)
        return carry

    def wd_block(cb):
        rows = pl.ds(64 + 16 * (cb % 2), 16)
        parts = [wrec[2 * i + cb // 2, rows, :] for i in range(16)]
        return jnp.concatenate(parts, axis=0)

    def run(first, last):
        lax.fori_loop(first, last, compute, 0)

    def pick(q, first, last):
        def body(r, carry):
            for c, sel in ((1, xs), (2, gs)):
                choose(q, r, c, me, sel.at[q * 8 + r])
            return carry

        lax.fori_loop(first, last, body, 0)

    def raw_copy(q, way, k):
        cols = pl.ds(*XC[k if k < 2 else way])
        if k == 2:
            src, dst = cbuf.at[q * 8 + 7, :, cols], near.at[q, way, :, cols]
        elif k == 3:
            src, dst = near.at[q, way, :, cols], far.at[q, way, :, cols]
        else:
            src, dst = cbuf.at[q * 8 + slot(3, 1 - way), :, cols], raw.at[q, way, :, cols]
        return pltpu.make_async_remote_copy(
            src_ref=src,
            dst_ref=dst,
            send_sem=r_send.at[q, way, k],
            recv_sem=r_recv.at[q, way, k],
            device_id=(n, ring[way]),
            device_id_type=MESH,
        )

    def across(r, leg):
        return pltpu.make_async_remote_copy(
            src_ref=zf.at[r] if leg else cbuf.at[8 + r, :, pl.ds(XW, D - XW)],
            dst_ref=cm.at[r] if leg else zf.at[r],
            send_sem=f_send.at[r, leg],
            recv_sem=f_recv.at[r, leg],
            device_id=(lax.rem(n + NODES // 2, NODES), zside[r % 2]),
            device_id_type=MESH,
        )

    def hand_across(first, last):
        for r in range(first, last):
            across(r, 0).wait_recv()
            across(r, 1).start()

    for c in range(3):
        for way in range(2):
            gather(0, way, 1, c).start()
    for c in range(3):
        to_mate(c, 0).start()
    for c in locals_:
        c.wait()
    mixed[n] = pack[n // 2, lax.rem(n, 2)]
    for c in owns:
        c.wait()
    pick(0, 0, 1)
    for c in range(2):
        arrive(0, 1, c)
    for c in range(2):
        to_mate(c, 0).wait_recv()
        to_mate(c, 1).start()
    arrive(0, 1, 2)
    to_mate(2, 0).wait_recv()
    to_mate(2, 1).start()
    each_peer(lambda k: spread(k).start())
    pick(0, 1, 3)
    for c in range(3):
        arrive(0, 2, c)
    pick(0, 3, 5)
    for c in range(2):
        arrive(0, 3, c)
    for c in range(2):
        to_mate(c, 1).wait_recv()
        for way in range(2):
            gather(1, way, 1, c).start()
    arrive(0, 3, 2)
    to_mate(2, 1).wait_recv()
    for way in range(2):
        gather(1, way, 1, 2).start()
    pick(1, 0, 1)
    for c in range(3):
        arrive(0, 4, c)
    each_peer(lambda k: spread(k).wait_recv())

    def forward(k):
        to = flip(k)
        stage[to] = mixed[partner[to]]
        collect(k).start()

    each_peer(forward)
    wrec[n] = mixed[partner[n]]
    for c in range(3):
        arrive(1, 1, c)
    pick(1, 1, 3)
    for c in range(3):
        arrive(1, 2, c)
    pick(1, 3, 5)
    each_peer(lambda k: collect(k).wait_recv())
    run(0, 2)
    for c in range(2):
        arrive(1, 3, c)
    run(2, 4)
    arrive(1, 3, 2)
    for way in range(2):
        for k in (2, 0, 1):
            raw_copy(0, way, k).start()
    run(4, 6)
    for r in range(4):
        across(r, 0).start()
    run(6, 7)
    for r in range(4, 6):
        across(r, 0).start()
    for c in range(3):
        arrive(1, 4, c)
    run(7, 8)

    outs = [
        pltpu.make_async_copy(dg_v, dg_out, out_sem.at[0]),
        pltpu.make_async_copy(du_v, du_out, out_sem.at[1]),
        pltpu.make_async_copy(dd_v, dd_out, out_sem.at[2]),
        pltpu.make_async_copy(dt_v, dt_out, out_sem.at[3]),
    ]

    def grad_piece(i):
        cols = pl.ds(256 * (i % 4), 256)
        if i < 4:
            x = xs[:, :, cols].reshape(GROUP * BLK, 256)
            both = tn(x, gact[...].reshape(GROUP * BLK, 2 * H))
            dg_v[cols, :] = both[:, :H].astype(BF)
            du_v[cols, :] = both[:, H:].astype(BF)
        else:
            g = gs[:, :, cols].reshape(GROUP * BLK, 256)
            dd_v[:, cols] = tn(hact[...].reshape(GROUP * BLK, H), g).astype(BF)
        if i == 3:
            outs[0].start()
            outs[1].start()
        if i == 7:
            outs[2].start()

    def placed(block, row):
        second = jnp.concatenate([row] * (block.shape[1] // 128), axis=1)
        block = block.astype(F32)
        return [block * (1.0 - second), block * second]

    def plus(left, right):
        return [u + v for u, v in zip(left, right)]

    def mine(q, r, cols):
        return placed(cbuf[q * 8 + r, :, pl.ds(*cols)], row_of(q, r, me))

    def ours(r, cols):
        other = placed(cm[r, :, pl.ds(cols[0] - XW, cols[1])], row_of(0, r, mate))
        return plus(mine(0, r, cols), other)

    def back_copy(q, way, hops, c):
        cols = pl.ds(*XC[c])
        return pltpu.make_async_remote_copy(
            src_ref=sbuf.at[q, way, :, :, cols] if hops == 2 else rbuf.at[q, way, 1, :, :, cols],
            dst_ref=rbuf.at[q, way, hops - 1, :, :, cols],
            send_sem=rs_send.at[q, way, hops - 1, c],
            recv_sem=rs_recv.at[q, way, hops - 1, c],
            device_id=(n, ring[way]),
            device_id_type=MESH,
        )

    def back_send(q, way, hops, c):
        r = slot(hops, 1 - way)
        cols = pl.ds(*XC[c])
        sums = mine(q, r, XC[c])
        if hops == 2:
            raw_copy(q, way, c).wait_recv()
            sums = plus(sums, placed(raw[q, way, :, cols], row_of(q, r, ring[1 - way])))
            if c == way:
                raw_copy(q, way, 3).wait_recv()
                sums = plus(sums, placed(far[q, way, :, cols], row_of(q, r, beyond[1 - way])))
            for b in range(2):
                sbuf[q, way, b, :, cols] = sums[b].astype(BF)
        else:
            back_copy(q, way, 2, c).wait_recv()
            for b in range(2):
                rbuf[q, way, 1, b, :, cols] = (
                    rbuf[q, way, 1, b, :, cols].astype(F32) + sums[b]
                ).astype(BF)
        back_copy(q, way, hops, c).start()

    def total(q, c):
        cols = pl.ds(*XC[c])
        sums = mine(q, 0, XC[c])
        for way in range(2):
            back_copy(q, way, 1, c).wait_recv()
            sums = plus(sums, [rbuf[q, way, 0, b, :, cols].astype(F32) for b in range(2)])
        return sums

    def joint_copy(way, hops, c):
        cols = pl.ds(ZC[c][0] - XW, ZC[c][1])
        fresh = hops == 4 or (hops == 3 and c != way)
        return pltpu.make_async_remote_copy(
            src_ref=zst.at[way, 4 - hops, :, :, cols] if fresh else zr.at[way, hops, :, :, cols],
            dst_ref=zr.at[way, hops - 1, :, :, cols],
            send_sem=t_send.at[way, hops - 1, c],
            recv_sem=t_recv.at[way, hops - 1, c],
            device_id=(n, ring[way]),
            device_id_type=MESH,
        )

    def joint_send(way, hops, c):
        cols = pl.ds(ZC[c][0] - XW, ZC[c][1])
        sums = ours(slot(hops, 1 - way), ZC[c])
        if hops == 4 or (hops == 3 and c != way):
            for b in range(2):
                zst[way, 4 - hops, b, :, cols] = sums[b].astype(BF)
        else:
            joint_copy(way, hops + 1, c).wait_recv()
            for b in range(2):
                zr[way, hops, b, :, cols] = (
                    zr[way, hops, b, :, cols].astype(F32) + sums[b]
                ).astype(BF)
        joint_copy(way, hops, c).start()

    def z_copy(c, leg):
        cols = pl.ds(*XC[c])
        return pltpu.make_async_remote_copy(
            src_ref=zl.at[:, :, cols] if leg else zsend.at[:, :, cols],
            dst_ref=zrecv.at[:, :, cols] if leg else zl.at[:, :, cols],
            send_sem=z_send.at[c, leg],
            recv_sem=z_recv.at[c, leg],
            device_id=(lax.rem(n + NODES // 2, NODES), zside[c]),
            device_id_type=MESH,
        )

    for way in range(2):
        for k in (2, 0, 1):
            raw_copy(1, way, k).start()
    for r in range(6, 8):
        across(r, 0).start()
    grad_piece(0)
    hand_across(0, 4)
    for q in (1, 0):
        for way in range(2):
            raw_copy(q, way, 2).wait_recv()
            raw_copy(q, way, 3).start()
    grad_piece(1)
    for i, (q, hops) in enumerate(((1, 2), (0, 2), (1, 1), (0, 1))):
        for turn in range(2):
            for way in range(2):
                back_send(q, way, hops, way ^ turn)
            if i < 3:
                grad_piece(2 + 2 * i + turn)
        if i == 0:
            hand_across(4, 6)
        if i == 1:
            hand_across(6, 8)
    for c in range(2):
        sums = total(1, c)
        for b in range(2):
            zsend[b, :, pl.ds(*XC[c])] = sums[b].astype(BF)
        z_copy(c, 0).start()
    for r in (7, 5, 6, 3, 4, 1, 2, 0):
        across(r, 1).wait_recv()
        if r == 7:
            for way in range(2):
                joint_send(way, 4, way)
    for turn in range(2):
        for way in range(2):
            joint_send(way, 3, way ^ 1 ^ turn)
    for c in range(2):
        z_copy(c, 0).wait_recv()
        z_copy(c, 1).start()
    for hops in (2, 1):
        for turn in range(2):
            for way in range(2):
                joint_send(way, hops, way ^ 1 ^ turn)
    for c in range(2):
        sums = total(0, c)
        z_copy(c, 1).wait_recv()
        for b in range(2):
            dt_v[pl.ds(BLK * b, BLK), pl.ds(*XC[c])] = (
                sums[b] + zrecv[b, :, pl.ds(*XC[c])].astype(F32)
            ).astype(BF)
    for c in (1, 0):
        cols = pl.ds(ZC[c][0] - XW, ZC[c][1])
        sums = ours(0, ZC[c])
        for way in range(2):
            joint_copy(way, 1, c).wait_recv()
            sums = plus(sums, [zr[way, 0, b, :, cols].astype(F32) for b in range(2)])
        for b in range(2):
            dt_v[pl.ds(BLK * b, BLK), pl.ds(*ZC[c])] = sums[b].astype(BF)
    outs[3].start()

    for q in range(2):
        for way in range(2):
            for c in range(3):
                gather(q, way, 1, c).wait_send()
                gather(q, way, 2, c).wait_send()
                cut_copy(q, way, c).wait_send()
            gather(q, way, 3, 0).wait_send()
            if way == 0:
                gather(q, way, 4, 0).wait_send()
            last_copy(q, way).wait_send()
            for k in range(4):
                raw_copy(q, way, k).wait_send()
            for hops in (2, 1):
                for c in range(2):
                    back_copy(q, way, hops, c).wait_send()
    for c in range(3):
        for leg in range(2):
            to_mate(c, leg).wait_send()
    each_peer(lambda k: spread(k).wait_send())
    each_peer(lambda k: collect(k).wait_send())
    for c in range(2):
        for leg in range(2):
            z_copy(c, leg).wait_send()
    for r in range(8):
        for leg in range(2):
            across(r, leg).wait_send()
    for way in range(2):
        joint_copy(way, 4, way).wait_send()
        for hops in (3, 2, 1):
            for c in range(2):
                joint_copy(way, hops, c).wait_send()
    for c in outs:
        c.wait()


def on_device(tokens, grad_out, router_gate, counts, routes, partner, w_gate, w_up, w_down):
    groups = jnp.arange(GROUP, dtype=jnp.int32)
    live = jnp.arange(2, dtype=jnp.int32) < counts[0]
    gates = router_gate.T.reshape(4, 2, 1, BLK)
    hot = (routes[0].T[:, :, None] == groups) & live[None, :, None]
    signed = gates * jnp.array([1.0, -1.0], F32)[None, :, None, None]
    meta = jnp.sum(jnp.where(hot[:, :, :, None], signed, 0.0), axis=(0, 1))

    any_ = pl.BlockSpec(memory_space=pl.ANY)
    dma = pltpu.SemaphoreType.DMA
    shape = jax.ShapeDtypeStruct
    outs = pl.pallas_call(
        kernel,
        out_shape=(
            shape((2 * BLK, D), BF), shape((D, H), BF), shape((D, H), BF), shape((H, D), BF),
        ),
        in_specs=[pl.BlockSpec(memory_space=pltpu.SMEM)] + [any_] * 6,
        out_specs=[any_] * 4,
        scratch_shapes=[
            pltpu.VMEM((2, 8, GROUP, BLK), F32),
            pltpu.VMEM((2, 5, 2 * BLK, D), BF),
            pltpu.VMEM((2, 5, 2 * BLK, D), BF),
            pltpu.VMEM((16, BLK, D), BF),
            pltpu.VMEM((16, BLK, D), BF),
            pltpu.VMEM((16, BLK, 2 * H), BF),
            pltpu.VMEM((16, BLK, H), BF),
            pltpu.VMEM((16, BLK, D), BF),
            pltpu.VMEM((2, 2, 3, BLK, D), BF),
            pltpu.VMEM((2, 2, BLK, D), BF),
            pltpu.VMEM((2, 2 * BLK, D), BF),
            pltpu.VMEM((GROUP, BLK), F32),
            pltpu.VMEM((2, 2, BLK, XW), BF),
            pltpu.VMEM((2, 2, BLK, XW), BF),
            pltpu.VMEM((2, 2, BLK, XW), BF),
            pltpu.VMEM((2, 2, 2, BLK, XW), BF),
            pltpu.VMEM((2, 2, 2, 2, BLK, XW), BF),
            pltpu.VMEM((2, 2, 2, BLK, D - XW), BF),
            pltpu.VMEM((2, 4, 2, BLK, D - XW), BF),
            pltpu.VMEM((8, BLK, D - XW), BF),
            pltpu.VMEM((8, BLK, D - XW), BF),
            pltpu.VMEM((2, BLK, XW), BF),
            pltpu.VMEM((2, BLK, XW), BF),
            pltpu.VMEM((2, BLK, XW), BF),
            pltpu.VMEM((16, 2, PART, H), BF),
            pltpu.VMEM((NODES, PART, H), BF),
            pltpu.VMEM((NODES, PART, H), BF),
            pltpu.VMEM((NODES, PART, H), BF),
            pltpu.VMEM((D, H), BF),
            pltpu.VMEM((D, H), BF),
            pltpu.VMEM((H, D), BF),
            pltpu.VMEM((2 * BLK, D), BF),
            dma((2, 2, 4, 3)), dma((2, 2, 4, 3)), dma((2, 2, 4)), dma((2, 2, 4)), dma((3, 2)), dma((3, 2)),
            dma((NODES,)), dma((NODES,)), dma((NODES,)), dma((NODES,)),
            dma((2, 2, 4)), dma((2, 2, 4)), dma((2, 2, 2, 2)), dma((2, 2, 2, 2)), dma((2, 4, 2)), dma((2, 4, 2)),
            dma((8, 2)), dma((8, 2)), dma((2, 2)), dma((2, 2)), dma((9,)), dma((4,)),
        ],
        compiler_params=pltpu.CompilerParams(
            collective_id=0, has_side_effects=True, vmem_limit_bytes=67043328
        ),
        name="moe_step",
    )(
        partner, meta, tokens, grad_out,
        w_gate.reshape(16, 2, 32, H), w_up.reshape(16, 2, 32, H), w_down.reshape(16, 16, D),
    )
    dt, dg, du, dd = outs
    return dt, dg.reshape(1, D, H), du.reshape(1, D, H), dd.reshape(1, H, D)


def solution(mesh):
    rows = P(("node", "group"), None)
    cube = P(("node", "group"), None, None)
    return jax.shard_map(
        on_device,
        mesh=mesh,
        in_specs=(rows, rows, rows, P(("node", "group")), cube, P(), cube, cube, cube),
        out_specs=(rows, cube, cube, cube),
        check_vma=False,
    )
```

```python
import functools

import jax
import jax.numpy as jnp
from jax import lax
from jax.experimental import pallas as pl
from jax.experimental.pallas import tpu as pltpu
from jax.sharding import PartitionSpec as P

BF = jnp.bfloat16
F32 = jnp.float32
MESH = pl.DeviceIdType.MESH
NODES = 32
GROUP = 16
RING = 8
BLK = 128
D = 1024
H = 256
XW = 768
XC = ((0, 384), (384, 384))
ZC = ((768, 128), (896, 128))
PART = 96


def slot(hops, way):
    if hops == 0:
        return 0
    return 7 if hops == RING // 2 else 2 * hops - 1 + way


def nt(left, right):
    return lax.dot_general(left, right, (((1,), (1,)), ((), ())), preferred_element_type=F32)


def tn(left, right):
    return lax.dot_general(left, right, (((0,), (0,)), ((), ())), preferred_element_type=F32)


def kernel(
    partner, routes, counts, gates_in, tok_in, gr_in, wg_in, wu_in, wd_in,
    dt_out, dg_out, du_out, dd_out,
    gates, meta, tok, gr, xs, gs, gact, hact, cbuf, cut, relay, zrel, zmeta,
    raw, near, far, sbuf, rbuf, zst, zr, zf, cm, zsend, zl, zrecv,
    pack, mixed, stage, wrec, dg_v, du_v, dd_v, dt_v,
    g_send, g_recv, s_send, s_recv, m_send, m_recv, wa_send, wa_recv, wb_send, wb_recv,
    r_send, r_recv, rs_send, rs_recv, t_send, t_recv, f_send, f_recv, z_send, z_recv, loc, out_sem,
):
    n = lax.axis_index("node")
    me = lax.axis_index("group")
    y = me // 2
    side = me % 2
    ring = (lax.rem(y + 1, RING) * 2 + side, lax.rem(y + RING - 1, RING) * 2 + side)
    mate = y * 2 + (1 - side)
    turned = (n >= NODES // 2).astype(jnp.int32)
    zside = (y * 2 + lax.rem(side + turned, 2), y * 2 + lax.rem(side + 1 - turned, 2))
    beyond = (lax.rem(y + 2, RING) * 2 + side, lax.rem(y + RING - 2, RING) * 2 + side)

    locals_ = [
        pltpu.make_async_copy(wg_in, pack.at[:, :, pl.ds(0, 32), :], loc.at[0]),
        pltpu.make_async_copy(wu_in, pack.at[:, :, pl.ds(32, 32), :], loc.at[1]),
    ]
    for cb in range(4):
        locals_.append(
            pltpu.make_async_copy(
                wd_in.at[:, :, pl.ds(256 * cb, 256)],
                pack.at[:, cb // 2, pl.ds(64 + 16 * (cb % 2), 16), :],
                loc.at[2 + cb],
            )
        )
    owns = [
        pltpu.make_async_copy(gates_in, gates, loc.at[6]),
        pltpu.make_async_copy(tok_in, tok.at[0, 0], loc.at[7]),
        pltpu.make_async_copy(gr_in, gr.at[0, 0], loc.at[8]),
    ]
    for c in owns + locals_:
        c.start()

    barrier = pltpu.get_barrier_semaphore()

    def greet(k, carry):
        pl.semaphore_signal(
            barrier, inc=1, device_id=(lax.rem(n + k, NODES), me), device_id_type=MESH
        )
        return carry

    for g in ring:
        pl.semaphore_signal(barrier, inc=1, device_id=(n, g), device_id_type=MESH)
    lax.fori_loop(1, NODES, greet, 0)
    pl.semaphore_signal(
        barrier, inc=1, device_id=(lax.rem(n + NODES // 2, NODES), mate), device_id_type=MESH
    )

    owns[0].wait()
    device = lax.broadcasted_iota(jnp.int32, (GROUP, BLK), 0)
    table = jnp.zeros((GROUP, BLK), F32)
    for b in range(2):
        for k in range(4):
            asked = jnp.where(b < counts[0], routes[b, k], -1)
            weights = gates[pl.ds(k, 1), pl.ds(BLK * b, BLK)]
            table = jnp.where(device == asked, -weights if b else weights, table)
    meta[0, 0] = table
    pl.semaphore_wait(barrier, NODES - 1 + 3)

    bufs = (meta, tok, gr)
    ins = (meta.at[0, 0], tok_in, gr_in)

    def gather(q, way, hops, c):
        src = ins[c] if q == 0 and hops == 1 else bufs[c].at[q, slot(hops - 1, way)]
        return pltpu.make_async_remote_copy(
            src_ref=src,
            dst_ref=bufs[c].at[q, slot(hops, way)],
            send_sem=g_send.at[q, way, hops - 1, c],
            recv_sem=g_recv.at[q, way, hops - 1, c],
            device_id=(n, ring[way]),
            device_id_type=MESH,
        )

    def cut_copy(q, way, k):
        if k < 2:
            dst = (xs, gs)[k].at[q * 8 + slot(3, way)]
        else:
            dst = relay.at[q, way]
        return pltpu.make_async_remote_copy(
            src_ref=cut.at[q, way, k],
            dst_ref=dst,
            send_sem=s_send.at[q, way, k],
            recv_sem=s_recv.at[q, way, k],
            device_id=(n, ring[way]),
            device_id_type=MESH,
        )

    def last_copy(q, way):
        return pltpu.make_async_remote_copy(
            src_ref=relay.at[q, way],
            dst_ref=(xs, gs)[way].at[q * 8 + 7],
            send_sem=s_send.at[q, way, 3],
            recv_sem=s_recv.at[q, way, 3],
            device_id=(n, ring[way]),
            device_id_type=MESH,
        )

    def to_mate(c, leg):
        stop = zrel.at[c - 1] if c else zmeta
        return pltpu.make_async_remote_copy(
            src_ref=ins[c] if leg == 0 else stop,
            dst_ref=stop if leg == 0 else bufs[c].at[1, 0],
            send_sem=m_send.at[c, leg],
            recv_sem=m_recv.at[c, leg],
            device_id=(lax.rem(n + NODES // 2, NODES), zside[1 if c == 2 else 0]),
            device_id_type=MESH,
        )

    def flip(k):
        return sum(lax.rem(n // (1 << i) + k // (1 << i), 2) * (1 << i) for i in range(5))

    def spread(k):
        to = flip(k)
        return pltpu.make_async_remote_copy(
            src_ref=pack.at[to // 2, lax.rem(to, 2)],
            dst_ref=mixed.at[n],
            send_sem=wa_send.at[k],
            recv_sem=wa_recv.at[k],
            device_id=(to, me),
            device_id_type=MESH,
        )

    def collect(k):
        to = flip(k)
        return pltpu.make_async_remote_copy(
            src_ref=stage.at[to],
            dst_ref=wrec.at[n],
            send_sem=wb_send.at[k],
            recv_sem=wb_recv.at[k],
            device_id=(to, me),
            device_id_type=MESH,
        )

    def each_peer(act):
        def body(k, carry):
            act(k)
            return carry

        lax.fori_loop(1, NODES, body, 0)

    def row_of(q, r, who):
        return (meta[q, r, pl.ds(who, 1), :] < 0.0).astype(F32)

    def choose(q, r, c, who, dst):
        second = row_of(q, r, who)
        first = 1.0 - second
        for cb in range(D // 128):
            cols = pl.ds(128 * cb, 128)
            a = bufs[c][q, r, pl.ds(0, BLK), cols].astype(F32)
            b = bufs[c][q, r, pl.ds(BLK, BLK), cols].astype(F32)
            dst[:, cols] = (a * first + b * second).astype(BF)

    def arrive(q, hops, c):
        if hops == 1:
            for way in range(2):
                gather(q, way, 1, c).wait_recv()
                gather(q, way, 2, c).start()
        elif hops == 2:
            for way in range(2):
                gather(q, way, 2, c).wait_recv()
                if c == 0:
                    gather(q, way, 3, 0).start()
                    continue
                if c == 1 + way:
                    choose(q, slot(2, way), c, beyond[way], cut.at[q, way, 2])
                    cut_copy(q, way, 2).start()
                choose(q, slot(2, way), c, ring[way], cut.at[q, way, c - 1])
                cut_copy(q, way, c - 1).start()
        elif hops == 3:
            for way in range(2):
                if c == 0:
                    gather(q, way, 3, 0).wait_recv()
                    if way == 0:
                        gather(q, way, 4, 0).start()
                    continue
                if c == 1 + way:
                    cut_copy(q, way, 2).wait_recv()
                    last_copy(q, way).start()
                cut_copy(q, way, c - 1).wait_recv()
        elif c == 0:
            gather(q, 0, 4, 0).wait_recv()
        else:
            last_copy(q, c - 1).wait_recv()

    pick_me = (lax.broadcasted_iota(jnp.int32, (GROUP, 128), 0) == me).astype(F32)

    def compute(pair, carry):
        two = pl.ds(2 * pair, 2)
        x = xs[two].reshape(2 * BLK, D)
        wg = wrec[:, pl.ds(0, 32), :].reshape(D, H)
        wu = wrec[:, pl.ds(32, 32), :].reshape(D, H)
        gate_pre = jnp.dot(x, wg, preferred_element_type=F32)
        up_pre = jnp.dot(x, wu, preferred_element_type=F32)
        grad_hidden = None
        for cb in range(4):
            g = gs[two, :, pl.ds(256 * cb, 256)].reshape(2 * BLK, 256)
            w = wd_block(cb)
            term = nt(g, w)
            grad_hidden = term if grad_hidden is None else grad_hidden + term
        weight = jnp.concatenate(
            [
                lax.dot_general(
                    meta[pair // 4, 2 * lax.rem(pair, 4) + j], pick_me, (((0,), (0,)), ((), ())),
                    preferred_element_type=F32, precision=lax.Precision.HIGHEST,
                )
                for j in range(2)
            ],
            axis=0,
        )
        weight = jnp.abs(jnp.concatenate([weight, weight], axis=1))
        sig = 1.0 / (1.0 + jnp.exp(-gate_pre))
        swish = gate_pre * sig
        grad_hidden = grad_hidden * weight
        hact[two] = (swish * up_pre * weight).astype(BF).reshape(2, BLK, H)
        gu = (grad_hidden * swish).astype(BF)
        gg = (grad_hidden * up_pre * sig * (1.0 + gate_pre * (1.0 - sig))).astype(BF)
        gact[two, :, pl.ds(0, H)] = gg.reshape(2, BLK, H)
        gact[two, :, pl.ds(H, H)] = gu.reshape(2, BLK, H)
        back = nt(gg, wg) + nt(gu, wu)
        cbuf[two] = back.astype(BF).reshape(2, BLK, D)
        return carry

    def wd_block(cb):
        rows = pl.ds(64 + 16 * (cb % 2), 16)
        parts = [wrec[2 * i + cb // 2, rows, :] for i in range(16)]
        return jnp.concatenate(parts, axis=0)

    def run(first, last):
        lax.fori_loop(first, last, compute, 0)

    def pick(q, first, last):
        def body(r, carry):
            for c, sel in ((1, xs), (2, gs)):
                choose(q, r, c, me, sel.at[q * 8 + r])
            return carry

        lax.fori_loop(first, last, body, 0)

    def raw_copy(q, way, k):
        cols = pl.ds(*XC[k if k < 2 else way])
        if k == 2:
            src, dst = cbuf.at[q * 8 + 7, :, cols], near.at[q, way, :, cols]
        elif k == 3:
            src, dst = near.at[q, way, :, cols], far.at[q, way, :, cols]
        else:
            src, dst = cbuf.at[q * 8 + slot(3, 1 - way), :, cols], raw.at[q, way, :, cols]
        return pltpu.make_async_remote_copy(
            src_ref=src,
            dst_ref=dst,
            send_sem=r_send.at[q, way, k],
            recv_sem=r_recv.at[q, way, k],
            device_id=(n, ring[way]),
            device_id_type=MESH,
        )

    def across(r, leg):
        return pltpu.make_async_remote_copy(
            src_ref=zf.at[r] if leg else cbuf.at[8 + r, :, pl.ds(XW, D - XW)],
            dst_ref=cm.at[r] if leg else zf.at[r],
            send_sem=f_send.at[r, leg],
            recv_sem=f_recv.at[r, leg],
            device_id=(lax.rem(n + NODES // 2, NODES), zside[r % 2]),
            device_id_type=MESH,
        )

    def hand_across(first, last):
        for r in range(first, last):
            across(r, 0).wait_recv()
            across(r, 1).start()

    for c in range(3):
        for way in range(2):
            gather(0, way, 1, c).start()
    for c in range(3):
        to_mate(c, 0).start()
    for c in locals_:
        c.wait()
    mixed[n] = pack[n // 2, lax.rem(n, 2)]
    for c in owns[1:]:
        c.wait()
    pick(0, 0, 1)
    for c in range(2):
        arrive(0, 1, c)
    for c in range(2):
        to_mate(c, 0).wait_recv()
        to_mate(c, 1).start()
    arrive(0, 1, 2)
    to_mate(2, 0).wait_recv()
    to_mate(2, 1).start()
    each_peer(lambda k: spread(k).start())
    pick(0, 1, 3)
    for c in range(3):
        arrive(0, 2, c)
    pick(0, 3, 5)
    for c in range(2):
        arrive(0, 3, c)
    for c in range(2):
        to_mate(c, 1).wait_recv()
        for way in range(2):
            gather(1, way, 1, c).start()
    arrive(0, 3, 2)
    to_mate(2, 1).wait_recv()
    for way in range(2):
        gather(1, way, 1, 2).start()
    pick(1, 0, 1)
    for c in range(3):
        arrive(0, 4, c)
    each_peer(lambda k: spread(k).wait_recv())

    def forward(k):
        to = flip(k)
        stage[to] = mixed[partner[to]]
        collect(k).start()

    each_peer(forward)
    wrec[n] = mixed[partner[n]]
    for c in range(3):
        arrive(1, 1, c)
    pick(1, 1, 3)
    for c in range(3):
        arrive(1, 2, c)
    pick(1, 3, 5)
    each_peer(lambda k: collect(k).wait_recv())
    run(0, 2)
    for c in range(2):
        arrive(1, 3, c)
    run(2, 4)
    arrive(1, 3, 2)
    for way in range(2):
        for k in (2, 0, 1):
            raw_copy(0, way, k).start()
    run(4, 6)
    for r in range(4):
        across(r, 0).start()
    run(6, 7)
    for r in range(4, 6):
        across(r, 0).start()
    for c in range(3):
        arrive(1, 4, c)
    run(7, 8)

    outs = [
        pltpu.make_async_copy(dg_v, dg_out, out_sem.at[0]),
        pltpu.make_async_copy(du_v, du_out, out_sem.at[1]),
        pltpu.make_async_copy(dd_v, dd_out, out_sem.at[2]),
        pltpu.make_async_copy(dt_v, dt_out, out_sem.at[3]),
    ]

    def grad_piece(i):
        cols = pl.ds(256 * (i % 4), 256)
        if i < 4:
            x = xs[:, :, cols].reshape(GROUP * BLK, 256)
            both = tn(x, gact[...].reshape(GROUP * BLK, 2 * H))
            dg_v[cols, :] = both[:, :H].astype(BF)
            du_v[cols, :] = both[:, H:].astype(BF)
        else:
            g = gs[:, :, cols].reshape(GROUP * BLK, 256)
            dd_v[:, cols] = tn(hact[...].reshape(GROUP * BLK, H), g).astype(BF)
        if i == 3:
            outs[0].start()
            outs[1].start()
        if i == 7:
            outs[2].start()

    def placed(block, row):
        second = jnp.concatenate([row] * (block.shape[1] // 128), axis=1)
        block = block.astype(F32)
        return [block * (1.0 - second), block * second]

    def plus(left, right):
        return [u + v for u, v in zip(left, right)]

    def mine(q, r, cols):
        return placed(cbuf[q * 8 + r, :, pl.ds(*cols)], row_of(q, r, me))

    def ours(r, cols):
        other = placed(cm[r, :, pl.ds(cols[0] - XW, cols[1])], row_of(0, r, mate))
        return plus(mine(0, r, cols), other)

    def back_copy(q, way, hops, c):
        cols = pl.ds(*XC[c])
        return pltpu.make_async_remote_copy(
            src_ref=sbuf.at[q, way, :, :, cols] if hops == 2 else rbuf.at[q, way, 1, :, :, cols],
            dst_ref=rbuf.at[q, way, hops - 1, :, :, cols],
            send_sem=rs_send.at[q, way, hops - 1, c],
            recv_sem=rs_recv.at[q, way, hops - 1, c],
            device_id=(n, ring[way]),
            device_id_type=MESH,
        )

    def back_send(q, way, hops, c):
        r = slot(hops, 1 - way)
        cols = pl.ds(*XC[c])
        sums = mine(q, r, XC[c])
        if hops == 2:
            raw_copy(q, way, c).wait_recv()
            sums = plus(sums, placed(raw[q, way, :, cols], row_of(q, r, ring[1 - way])))
            if c == way:
                raw_copy(q, way, 3).wait_recv()
                sums = plus(sums, placed(far[q, way, :, cols], row_of(q, r, beyond[1 - way])))
            for b in range(2):
                sbuf[q, way, b, :, cols] = sums[b].astype(BF)
        else:
            back_copy(q, way, 2, c).wait_recv()
            for b in range(2):
                rbuf[q, way, 1, b, :, cols] = (
                    rbuf[q, way, 1, b, :, cols].astype(F32) + sums[b]
                ).astype(BF)
        back_copy(q, way, hops, c).start()

    def total(q, c):
        cols = pl.ds(*XC[c])
        sums = mine(q, 0, XC[c])
        for way in range(2):
            back_copy(q, way, 1, c).wait_recv()
            sums = plus(sums, [rbuf[q, way, 0, b, :, cols].astype(F32) for b in range(2)])
        return sums

    def joint_copy(way, hops, c):
        cols = pl.ds(ZC[c][0] - XW, ZC[c][1])
        fresh = hops == 4 or (hops == 3 and c != way)
        return pltpu.make_async_remote_copy(
            src_ref=zst.at[way, 4 - hops, :, :, cols] if fresh else zr.at[way, hops, :, :, cols],
            dst_ref=zr.at[way, hops - 1, :, :, cols],
            send_sem=t_send.at[way, hops - 1, c],
            recv_sem=t_recv.at[way, hops - 1, c],
            device_id=(n, ring[way]),
            device_id_type=MESH,
        )

    def joint_send(way, hops, c):
        cols = pl.ds(ZC[c][0] - XW, ZC[c][1])
        sums = ours(slot(hops, 1 - way), ZC[c])
        if hops == 4 or (hops == 3 and c != way):
            for b in range(2):
                zst[way, 4 - hops, b, :, cols] = sums[b].astype(BF)
        else:
            joint_copy(way, hops + 1, c).wait_recv()
            for b in range(2):
                zr[way, hops, b, :, cols] = (
                    zr[way, hops, b, :, cols].astype(F32) + sums[b]
                ).astype(BF)
        joint_copy(way, hops, c).start()

    def z_copy(c, leg):
        cols = pl.ds(*XC[c])
        return pltpu.make_async_remote_copy(
            src_ref=zl.at[:, :, cols] if leg else zsend.at[:, :, cols],
            dst_ref=zrecv.at[:, :, cols] if leg else zl.at[:, :, cols],
            send_sem=z_send.at[c, leg],
            recv_sem=z_recv.at[c, leg],
            device_id=(lax.rem(n + NODES // 2, NODES), zside[c]),
            device_id_type=MESH,
        )

    for way in range(2):
        for k in (2, 0, 1):
            raw_copy(1, way, k).start()
    for r in range(6, 8):
        across(r, 0).start()
    grad_piece(0)
    hand_across(0, 4)
    for q in (1, 0):
        for way in range(2):
            raw_copy(q, way, 2).wait_recv()
            raw_copy(q, way, 3).start()
    grad_piece(1)
    def ring_step(q, hops, turn):
        for way in range(2):
            back_send(q, way, hops, way ^ turn)

    def joint_step(hops):
        for turn in range(2):
            for way in range(2):
                joint_send(way, hops, way ^ 1 ^ turn)

    ring_step(1, 2, 0)
    grad_piece(2)
    ring_step(1, 2, 1)
    hand_across(4, 6)
    ring_step(0, 2, 0)
    grad_piece(3)
    hand_across(6, 8)
    ring_step(1, 1, 0)
    grad_piece(4)
    ring_step(1, 1, 1)
    for c in range(2):
        sums = total(1, c)
        for b in range(2):
            zsend[b, :, pl.ds(*XC[c])] = sums[b].astype(BF)
        z_copy(c, 0).start()
    ring_step(0, 2, 1)
    grad_piece(5)
    across(7, 1).wait_recv()
    for way in range(2):
        joint_send(way, 4, way)
    ring_step(0, 1, 0)
    grad_piece(6)
    for r in (5, 6):
        across(r, 1).wait_recv()
    joint_step(3)
    for c in range(2):
        z_copy(c, 0).wait_recv()
        z_copy(c, 1).start()
    ring_step(0, 1, 1)
    for r in (3, 4):
        across(r, 1).wait_recv()
    joint_step(2)
    for r in (1, 2):
        across(r, 1).wait_recv()
    joint_step(1)
    grad_piece(7)
    across(0, 1).wait_recv()
    for c in range(2):
        sums = total(0, c)
        z_copy(c, 1).wait_recv()
        for b in range(2):
            dt_v[pl.ds(BLK * b, BLK), pl.ds(*XC[c])] = (
                sums[b] + zrecv[b, :, pl.ds(*XC[c])].astype(F32)
            ).astype(BF)
    for c in (1, 0):
        cols = pl.ds(ZC[c][0] - XW, ZC[c][1])
        sums = ours(0, ZC[c])
        for way in range(2):
            joint_copy(way, 1, c).wait_recv()
            sums = plus(sums, [zr[way, 0, b, :, cols].astype(F32) for b in range(2)])
        for b in range(2):
            dt_v[pl.ds(BLK * b, BLK), pl.ds(*ZC[c])] = sums[b].astype(BF)
    outs[3].start()

    for q in range(2):
        for way in range(2):
            for c in range(3):
                gather(q, way, 1, c).wait_send()
                gather(q, way, 2, c).wait_send()
                cut_copy(q, way, c).wait_send()
            gather(q, way, 3, 0).wait_send()
            if way == 0:
                gather(q, way, 4, 0).wait_send()
            last_copy(q, way).wait_send()
            for k in range(4):
                raw_copy(q, way, k).wait_send()
            for hops in (2, 1):
                for c in range(2):
                    back_copy(q, way, hops, c).wait_send()
    for c in range(3):
        for leg in range(2):
            to_mate(c, leg).wait_send()
    each_peer(lambda k: spread(k).wait_send())
    each_peer(lambda k: collect(k).wait_send())
    for c in range(2):
        for leg in range(2):
            z_copy(c, leg).wait_send()
    for r in range(8):
        for leg in range(2):
            across(r, leg).wait_send()
    for way in range(2):
        joint_copy(way, 4, way).wait_send()
        for hops in (3, 2, 1):
            for c in range(2):
                joint_copy(way, hops, c).wait_send()
    for c in outs:
        c.wait()


def hand_out(a, b, c, d, w, x, y, z, va, vb, vc, vd, into, out):
    triples = ((a, va, w), (b, vb, x), (c, vc, y), (d, vd, z))
    parts = []
    for i, (src, mid, dst) in enumerate(triples):
        rows = src.shape[0] // 2
        for j in range(2):
            at = pl.ds(rows * j, rows)
            parts.append((
                pltpu.make_async_copy(src.at[at], mid.at[at], into.at[2 * i + j]),
                pltpu.make_async_copy(mid.at[at], dst.at[at], out.at[2 * i + j]),
            ))
    for first, second in parts:
        first.start()
    for first, second in parts:
        first.wait()
        second.start()
    for first, second in parts:
        second.wait()


def on_device(tokens, grad_out, router_gate, counts, routes, partner, w_gate, w_up, w_down):
    any_ = pl.BlockSpec(memory_space=pl.ANY)
    dma = pltpu.SemaphoreType.DMA
    shape = jax.ShapeDtypeStruct
    outs = pl.pallas_call(
        kernel,
        out_shape=(
            shape((2 * BLK, D), BF), shape((D, H), BF), shape((D, H), BF), shape((H, D), BF),
        ),
        in_specs=[pl.BlockSpec(memory_space=pltpu.SMEM)] * 3 + [any_] * 6,
        out_specs=[any_] * 4,
        scratch_shapes=[
            pltpu.VMEM((4, 2 * BLK), F32),
            pltpu.VMEM((2, 8, GROUP, BLK), F32),
            pltpu.VMEM((2, 5, 2 * BLK, D), BF),
            pltpu.VMEM((2, 5, 2 * BLK, D), BF),
            pltpu.VMEM((16, BLK, D), BF),
            pltpu.VMEM((16, BLK, D), BF),
            pltpu.VMEM((16, BLK, 2 * H), BF),
            pltpu.VMEM((16, BLK, H), BF),
            pltpu.VMEM((16, BLK, D), BF),
            pltpu.VMEM((2, 2, 3, BLK, D), BF),
            pltpu.VMEM((2, 2, BLK, D), BF),
            pltpu.VMEM((2, 2 * BLK, D), BF),
            pltpu.VMEM((GROUP, BLK), F32),
            pltpu.VMEM((2, 2, BLK, XW), BF),
            pltpu.VMEM((2, 2, BLK, XW), BF),
            pltpu.VMEM((2, 2, BLK, XW), BF),
            pltpu.VMEM((2, 2, 2, BLK, XW), BF),
            pltpu.VMEM((2, 2, 2, 2, BLK, XW), BF),
            pltpu.VMEM((2, 2, 2, BLK, D - XW), BF),
            pltpu.VMEM((2, 4, 2, BLK, D - XW), BF),
            pltpu.VMEM((8, BLK, D - XW), BF),
            pltpu.VMEM((8, BLK, D - XW), BF),
            pltpu.VMEM((2, BLK, XW), BF),
            pltpu.VMEM((2, BLK, XW), BF),
            pltpu.VMEM((2, BLK, XW), BF),
            pltpu.VMEM((16, 2, PART, H), BF),
            pltpu.VMEM((NODES, PART, H), BF),
            pltpu.VMEM((NODES, PART, H), BF),
            pltpu.VMEM((NODES, PART, H), BF),
            pltpu.VMEM((D, H), BF),
            pltpu.VMEM((D, H), BF),
            pltpu.VMEM((H, D), BF),
            pltpu.VMEM((2 * BLK, D), BF),
            dma((2, 2, 4, 3)), dma((2, 2, 4, 3)), dma((2, 2, 4)), dma((2, 2, 4)), dma((3, 2)), dma((3, 2)),
            dma((NODES,)), dma((NODES,)), dma((NODES,)), dma((NODES,)),
            dma((2, 2, 4)), dma((2, 2, 4)), dma((2, 2, 2, 2)), dma((2, 2, 2, 2)), dma((2, 4, 2)), dma((2, 4, 2)),
            dma((8, 2)), dma((8, 2)), dma((2, 2)), dma((2, 2)), dma((9,)), dma((4,)),
        ],
        compiler_params=pltpu.CompilerParams(
            collective_id=0, has_side_effects=True, vmem_limit_bytes=67043328
        ),
        name="moe_step",
    )(
        partner, routes.reshape(2, 4), counts, router_gate.T, tokens, grad_out,
        w_gate.reshape(16, 2, 32, H), w_up.reshape(16, 2, 32, H), w_down.reshape(16, 16, D),
    )
    dt, dg, du, dd = pl.pallas_call(
        hand_out,
        out_shape=tuple(shape(o.shape, BF) for o in outs),
        in_specs=[any_] * 4,
        out_specs=[any_] * 4,
        scratch_shapes=[pltpu.VMEM(o.shape, BF) for o in outs] + [dma((8,)), dma((8,))],
        name="hand_out",
    )(*outs)
    return dt, dg.reshape(1, D, H), du.reshape(1, D, H), dd.reshape(1, H, D)


def solution(mesh):
    rows = P(("node", "group"), None)
    cube = P(("node", "group"), None, None)
    return jax.shard_map(
        on_device,
        mesh=mesh,
        in_specs=(rows, rows, rows, P(("node", "group")), cube, P(), cube, cube, cube),
        out_specs=(rows, cube, cube, cube),
        check_vma=False,
    )
```

```python
import functools

import jax
import jax.numpy as jnp
from jax import lax
from jax.experimental import pallas as pl
from jax.experimental.pallas import tpu as pltpu
from jax.sharding import PartitionSpec as P

BF = jnp.bfloat16
F32 = jnp.float32
MESH = pl.DeviceIdType.MESH
NODES = 32
GROUP = 16
RING = 8
BLK = 128
D = 1024
H = 256
XW = 640
XC = ((0, 384), (384, 256))
ZC = ((640, 256), (896, 128))
PART = 96


def slot(hops, way):
    if hops == 0:
        return 0
    return 7 if hops == RING // 2 else 2 * hops - 1 + way


def nt(left, right):
    return lax.dot_general(left, right, (((1,), (1,)), ((), ())), preferred_element_type=F32)


def tn(left, right):
    return lax.dot_general(left, right, (((0,), (0,)), ((), ())), preferred_element_type=F32)


def kernel(
    partner, routes, counts, gates_in, tok_in, gr_in, wg_in, wu_in, wd_in,
    dt_out, dg_out, du_out, dd_out,
    gates, meta, tok, gr, xs, gs, gact, hact, cbuf, cut, relay, zrel, zmeta,
    raw, near, far, sbuf, rbuf, zst, zr, zf, cm, zsend, zl, zrecv,
    pack, mixed, stage, wrec, dg_v, du_v, dd_v, dt_v,
    g_send, g_recv, s_send, s_recv, m_send, m_recv, wa_send, wa_recv, wb_send, wb_recv,
    r_send, r_recv, rs_send, rs_recv, t_send, t_recv, f_send, f_recv, z_send, z_recv, loc, out_sem,
):
    n = lax.axis_index("node")
    me = lax.axis_index("group")
    y = me // 2
    side = me % 2
    ring = (lax.rem(y + 1, RING) * 2 + side, lax.rem(y + RING - 1, RING) * 2 + side)
    mate = y * 2 + (1 - side)
    turned = (n >= NODES // 2).astype(jnp.int32)
    zside = (y * 2 + lax.rem(side + turned, 2), y * 2 + lax.rem(side + 1 - turned, 2))
    beyond = (lax.rem(y + 2, RING) * 2 + side, lax.rem(y + RING - 2, RING) * 2 + side)

    locals_ = [
        pltpu.make_async_copy(wg_in, pack.at[:, :, pl.ds(0, 32), :], loc.at[0]),
        pltpu.make_async_copy(wu_in, pack.at[:, :, pl.ds(32, 32), :], loc.at[1]),
    ]
    for cb in range(4):
        locals_.append(
            pltpu.make_async_copy(
                wd_in.at[:, :, pl.ds(256 * cb, 256)],
                pack.at[:, cb // 2, pl.ds(64 + 16 * (cb % 2), 16), :],
                loc.at[2 + cb],
            )
        )
    owns = [
        pltpu.make_async_copy(gates_in, gates, loc.at[6]),
        pltpu.make_async_copy(tok_in, tok.at[0, 0], loc.at[7]),
        pltpu.make_async_copy(gr_in, gr.at[0, 0], loc.at[8]),
    ]
    for c in owns + locals_:
        c.start()

    barrier = pltpu.get_barrier_semaphore()

    def greet(k, carry):
        pl.semaphore_signal(
            barrier, inc=1, device_id=(lax.rem(n + k, NODES), me), device_id_type=MESH
        )
        return carry

    for g in ring:
        pl.semaphore_signal(barrier, inc=1, device_id=(n, g), device_id_type=MESH)
    lax.fori_loop(1, NODES, greet, 0)
    pl.semaphore_signal(
        barrier, inc=1, device_id=(lax.rem(n + NODES // 2, NODES), mate), device_id_type=MESH
    )

    owns[0].wait()
    device = lax.broadcasted_iota(jnp.int32, (GROUP, BLK), 0)
    table = jnp.zeros((GROUP, BLK), F32)
    for b in range(2):
        for k in range(4):
            asked = jnp.where(b < counts[0], routes[b, k], -1)
            weights = gates[pl.ds(k, 1), pl.ds(BLK * b, BLK)]
            table = jnp.where(device == asked, -weights if b else weights, table)
    meta[0, 0] = table
    pl.semaphore_wait(barrier, NODES - 1 + 3)

    bufs = (meta, tok, gr)
    ins = (meta.at[0, 0], tok_in, gr_in)

    def gather(q, way, hops, c):
        src = ins[c] if q == 0 and hops == 1 else bufs[c].at[q, slot(hops - 1, way)]
        return pltpu.make_async_remote_copy(
            src_ref=src,
            dst_ref=bufs[c].at[q, slot(hops, way)],
            send_sem=g_send.at[q, way, hops - 1, c],
            recv_sem=g_recv.at[q, way, hops - 1, c],
            device_id=(n, ring[way]),
            device_id_type=MESH,
        )

    def cut_copy(q, way, k):
        if k < 2:
            dst = (xs, gs)[k].at[q * 8 + slot(3, way)]
        else:
            dst = relay.at[q, way]
        return pltpu.make_async_remote_copy(
            src_ref=cut.at[q, way, k],
            dst_ref=dst,
            send_sem=s_send.at[q, way, k],
            recv_sem=s_recv.at[q, way, k],
            device_id=(n, ring[way]),
            device_id_type=MESH,
        )

    def last_copy(q, way):
        return pltpu.make_async_remote_copy(
            src_ref=relay.at[q, way],
            dst_ref=(xs, gs)[way].at[q * 8 + 7],
            send_sem=s_send.at[q, way, 3],
            recv_sem=s_recv.at[q, way, 3],
            device_id=(n, ring[way]),
            device_id_type=MESH,
        )

    def to_mate(c, leg):
        stop = zrel.at[c - 1] if c else zmeta
        return pltpu.make_async_remote_copy(
            src_ref=ins[c] if leg == 0 else stop,
            dst_ref=stop if leg == 0 else bufs[c].at[1, 0],
            send_sem=m_send.at[c, leg],
            recv_sem=m_recv.at[c, leg],
            device_id=(lax.rem(n + NODES // 2, NODES), zside[1 if c == 2 else 0]),
            device_id_type=MESH,
        )

    def flip(k):
        return sum(lax.rem(n // (1 << i) + k // (1 << i), 2) * (1 << i) for i in range(5))

    def spread(k):
        to = flip(k)
        return pltpu.make_async_remote_copy(
            src_ref=pack.at[to // 2, lax.rem(to, 2)],
            dst_ref=mixed.at[n],
            send_sem=wa_send.at[k],
            recv_sem=wa_recv.at[k],
            device_id=(to, me),
            device_id_type=MESH,
        )

    def collect(k):
        to = flip(k)
        return pltpu.make_async_remote_copy(
            src_ref=stage.at[to],
            dst_ref=wrec.at[n],
            send_sem=wb_send.at[k],
            recv_sem=wb_recv.at[k],
            device_id=(to, me),
            device_id_type=MESH,
        )

    def each_peer(act):
        def body(k, carry):
            act(k)
            return carry

        lax.fori_loop(1, NODES, body, 0)

    def row_of(q, r, who):
        return (meta[q, r, pl.ds(who, 1), :] < 0.0).astype(F32)

    def choose(q, r, c, who, dst):
        second = row_of(q, r, who)
        first = 1.0 - second
        for cb in range(D // 128):
            cols = pl.ds(128 * cb, 128)
            a = bufs[c][q, r, pl.ds(0, BLK), cols].astype(F32)
            b = bufs[c][q, r, pl.ds(BLK, BLK), cols].astype(F32)
            dst[:, cols] = (a * first + b * second).astype(BF)

    def arrive(q, hops, c):
        if hops == 1:
            for way in range(2):
                gather(q, way, 1, c).wait_recv()
                gather(q, way, 2, c).start()
        elif hops == 2:
            for way in range(2):
                gather(q, way, 2, c).wait_recv()
                if c == 0:
                    gather(q, way, 3, 0).start()
                    continue
                if c == 1 + way:
                    choose(q, slot(2, way), c, beyond[way], cut.at[q, way, 2])
                    cut_copy(q, way, 2).start()
                choose(q, slot(2, way), c, ring[way], cut.at[q, way, c - 1])
                cut_copy(q, way, c - 1).start()
        elif hops == 3:
            for way in range(2):
                if c == 0:
                    gather(q, way, 3, 0).wait_recv()
                    if way == 0:
                        gather(q, way, 4, 0).start()
                    continue
                if c == 1 + way:
                    cut_copy(q, way, 2).wait_recv()
                    last_copy(q, way).start()
                cut_copy(q, way, c - 1).wait_recv()
        elif c == 0:
            gather(q, 0, 4, 0).wait_recv()
        else:
            last_copy(q, c - 1).wait_recv()

    pick_me = (lax.broadcasted_iota(jnp.int32, (GROUP, 128), 0) == me).astype(F32)

    def compute(pair, carry):
        two = pl.ds(2 * pair, 2)
        x = xs[two].reshape(2 * BLK, D)
        wg = wrec[:, pl.ds(0, 32), :].reshape(D, H)
        wu = wrec[:, pl.ds(32, 32), :].reshape(D, H)
        gate_pre = jnp.dot(x, wg, preferred_element_type=F32)
        up_pre = jnp.dot(x, wu, preferred_element_type=F32)
        grad_hidden = None
        for cb in range(4):
            g = gs[two, :, pl.ds(256 * cb, 256)].reshape(2 * BLK, 256)
            w = wd_block(cb)
            term = nt(g, w)
            grad_hidden = term if grad_hidden is None else grad_hidden + term
        weight = jnp.concatenate(
            [
                lax.dot_general(
                    meta[pair // 4, 2 * lax.rem(pair, 4) + j], pick_me, (((0,), (0,)), ((), ())),
                    preferred_element_type=F32, precision=lax.Precision.HIGHEST,
                )
                for j in range(2)
            ],
            axis=0,
        )
        weight = jnp.abs(jnp.concatenate([weight, weight], axis=1))
        sig = 1.0 / (1.0 + jnp.exp(-gate_pre))
        swish = gate_pre * sig
        grad_hidden = grad_hidden * weight
        hact[two] = (swish * up_pre * weight).astype(BF).reshape(2, BLK, H)
        gu = (grad_hidden * swish).astype(BF)
        gg = (grad_hidden * up_pre * sig * (1.0 + gate_pre * (1.0 - sig))).astype(BF)
        gact[two, :, pl.ds(0, H)] = gg.reshape(2, BLK, H)
        gact[two, :, pl.ds(H, H)] = gu.reshape(2, BLK, H)
        back = nt(gg, wg) + nt(gu, wu)
        cbuf[two] = back.astype(BF).reshape(2, BLK, D)
        return carry

    def wd_block(cb):
        rows = pl.ds(64 + 16 * (cb % 2), 16)
        parts = [wrec[2 * i + cb // 2, rows, :] for i in range(16)]
        return jnp.concatenate(parts, axis=0)

    def run(first, last):
        lax.fori_loop(first, last, compute, 0)

    def pick(q, first, last):
        def body(r, carry):
            for c, sel in ((1, xs), (2, gs)):
                choose(q, r, c, me, sel.at[q * 8 + r])
            return carry

        lax.fori_loop(first, last, body, 0)

    def raw_copy(q, way, k):
        cols = pl.ds(*XC[k if k < 2 else way])
        if k == 2:
            src, dst = cbuf.at[q * 8 + 7, :, cols], near.at[q, way, :, cols]
        elif k == 3:
            src, dst = near.at[q, way, :, cols], far.at[q, way, :, cols]
        else:
            src, dst = cbuf.at[q * 8 + slot(3, 1 - way), :, cols], raw.at[q, way, :, cols]
        return pltpu.make_async_remote_copy(
            src_ref=src,
            dst_ref=dst,
            send_sem=r_send.at[q, way, k],
            recv_sem=r_recv.at[q, way, k],
            device_id=(n, ring[way]),
            device_id_type=MESH,
        )

    def across(r, leg):
        return pltpu.make_async_remote_copy(
            src_ref=zf.at[r] if leg else cbuf.at[8 + r, :, pl.ds(XW, D - XW)],
            dst_ref=cm.at[r] if leg else zf.at[r],
            send_sem=f_send.at[r, leg],
            recv_sem=f_recv.at[r, leg],
            device_id=(lax.rem(n + NODES // 2, NODES), zside[r % 2]),
            device_id_type=MESH,
        )

    def hand_across(first, last):
        for r in range(first, last):
            across(r, 0).wait_recv()
            across(r, 1).start()

    for c in range(3):
        for way in range(2):
            gather(0, way, 1, c).start()
    for c in range(3):
        to_mate(c, 0).start()
    for c in locals_:
        c.wait()
    mixed[n] = pack[n // 2, lax.rem(n, 2)]
    for c in owns[1:]:
        c.wait()
    pick(0, 0, 1)
    for c in range(2):
        arrive(0, 1, c)
    for c in range(2):
        to_mate(c, 0).wait_recv()
        to_mate(c, 1).start()
    arrive(0, 1, 2)
    to_mate(2, 0).wait_recv()
    to_mate(2, 1).start()
    each_peer(lambda k: spread(k).start())
    pick(0, 1, 3)
    for c in range(3):
        arrive(0, 2, c)
    pick(0, 3, 5)
    for c in range(2):
        arrive(0, 3, c)
    for c in range(2):
        to_mate(c, 1).wait_recv()
        for way in range(2):
            gather(1, way, 1, c).start()
    arrive(0, 3, 2)
    to_mate(2, 1).wait_recv()
    for way in range(2):
        gather(1, way, 1, 2).start()
    pick(1, 0, 1)
    for c in range(3):
        arrive(0, 4, c)
    each_peer(lambda k: spread(k).wait_recv())

    def forward(k):
        to = flip(k)
        stage[to] = mixed[partner[to]]
        collect(k).start()

    each_peer(forward)
    wrec[n] = mixed[partner[n]]
    for c in range(3):
        arrive(1, 1, c)
    pick(1, 1, 3)
    for c in range(3):
        arrive(1, 2, c)
    pick(1, 3, 5)
    each_peer(lambda k: collect(k).wait_recv())
    run(4, 6)
    for r in range(4):
        across(r, 0).start()
    for c in range(2):
        arrive(1, 3, c)
    run(0, 2)
    arrive(1, 3, 2)
    run(2, 4)
    for way in range(2):
        for k in (2, 0, 1):
            raw_copy(0, way, k).start()
    run(6, 7)
    for r in range(4, 6):
        across(r, 0).start()
    hand_across(0, 4)
    for c in range(3):
        arrive(1, 4, c)
    run(7, 8)

    outs = [
        pltpu.make_async_copy(dg_v, dg_out, out_sem.at[0]),
        pltpu.make_async_copy(du_v, du_out, out_sem.at[1]),
        pltpu.make_async_copy(dd_v, dd_out, out_sem.at[2]),
        pltpu.make_async_copy(dt_v, dt_out, out_sem.at[3]),
    ]

    def grad_piece(i):
        cols = pl.ds(256 * (i % 4), 256)
        if i < 4:
            x = xs[:, :, cols].reshape(GROUP * BLK, 256)
            both = tn(x, gact[...].reshape(GROUP * BLK, 2 * H))
            dg_v[cols, :] = both[:, :H].astype(BF)
            du_v[cols, :] = both[:, H:].astype(BF)
        else:
            g = gs[:, :, cols].reshape(GROUP * BLK, 256)
            dd_v[:, cols] = tn(hact[...].reshape(GROUP * BLK, H), g).astype(BF)
        if i == 3:
            outs[0].start()
            outs[1].start()
        if i == 7:
            outs[2].start()

    def placed(block, row):
        second = jnp.concatenate([row] * (block.shape[1] // 128), axis=1)
        block = block.astype(F32)
        return [block * (1.0 - second), block * second]

    def plus(left, right):
        return [u + v for u, v in zip(left, right)]

    def mine(q, r, cols):
        return placed(cbuf[q * 8 + r, :, pl.ds(*cols)], row_of(q, r, me))

    def ours(r, cols):
        other = placed(cm[r, :, pl.ds(cols[0] - XW, cols[1])], row_of(0, r, mate))
        return plus(mine(0, r, cols), other)

    def back_copy(q, way, hops, c):
        cols = pl.ds(*XC[c])
        return pltpu.make_async_remote_copy(
            src_ref=sbuf.at[q, way, :, :, cols] if hops == 2 else rbuf.at[q, way, 1, :, :, cols],
            dst_ref=rbuf.at[q, way, hops - 1, :, :, cols],
            send_sem=rs_send.at[q, way, hops - 1, c],
            recv_sem=rs_recv.at[q, way, hops - 1, c],
            device_id=(n, ring[way]),
            device_id_type=MESH,
        )

    def back_send(q, way, hops, c):
        r = slot(hops, 1 - way)
        cols = pl.ds(*XC[c])
        sums = mine(q, r, XC[c])
        if hops == 2:
            raw_copy(q, way, c).wait_recv()
            sums = plus(sums, placed(raw[q, way, :, cols], row_of(q, r, ring[1 - way])))
            if c == way:
                raw_copy(q, way, 3).wait_recv()
                sums = plus(sums, placed(far[q, way, :, cols], row_of(q, r, beyond[1 - way])))
            for b in range(2):
                sbuf[q, way, b, :, cols] = sums[b].astype(BF)
        else:
            back_copy(q, way, 2, c).wait_recv()
            for b in range(2):
                rbuf[q, way, 1, b, :, cols] = (
                    rbuf[q, way, 1, b, :, cols].astype(F32) + sums[b]
                ).astype(BF)
        back_copy(q, way, hops, c).start()

    def total(q, c):
        cols = pl.ds(*XC[c])
        sums = mine(q, 0, XC[c])
        for way in range(2):
            back_copy(q, way, 1, c).wait_recv()
            sums = plus(sums, [rbuf[q, way, 0, b, :, cols].astype(F32) for b in range(2)])
        return sums

    def joint_copy(way, hops, c):
        cols = pl.ds(ZC[c][0] - XW, ZC[c][1])
        fresh = hops == 4 or (hops == 3 and c != way)
        return pltpu.make_async_remote_copy(
            src_ref=zst.at[way, 4 - hops, :, :, cols] if fresh else zr.at[way, hops, :, :, cols],
            dst_ref=zr.at[way, hops - 1, :, :, cols],
            send_sem=t_send.at[way, hops - 1, c],
            recv_sem=t_recv.at[way, hops - 1, c],
            device_id=(n, ring[way]),
            device_id_type=MESH,
        )

    def joint_send(way, hops, c):
        cols = pl.ds(ZC[c][0] - XW, ZC[c][1])
        sums = ours(slot(hops, 1 - way), ZC[c])
        if hops == 4 or (hops == 3 and c != way):
            for b in range(2):
                zst[way, 4 - hops, b, :, cols] = sums[b].astype(BF)
        else:
            joint_copy(way, hops + 1, c).wait_recv()
            for b in range(2):
                zr[way, hops, b, :, cols] = (
                    zr[way, hops, b, :, cols].astype(F32) + sums[b]
                ).astype(BF)
        joint_copy(way, hops, c).start()

    def z_copy(c, leg):
        cols = pl.ds(*XC[c])
        return pltpu.make_async_remote_copy(
            src_ref=zl.at[:, :, cols] if leg else zsend.at[:, :, cols],
            dst_ref=zrecv.at[:, :, cols] if leg else zl.at[:, :, cols],
            send_sem=z_send.at[c, leg],
            recv_sem=z_recv.at[c, leg],
            device_id=(lax.rem(n + NODES // 2, NODES), zside[c]),
            device_id_type=MESH,
        )

    for way in range(2):
        for k in (2, 0, 1):
            raw_copy(1, way, k).start()
    for r in range(6, 8):
        across(r, 0).start()
    grad_piece(0)
    for q in (1, 0):
        for way in range(2):
            raw_copy(q, way, 2).wait_recv()
            raw_copy(q, way, 3).start()
    grad_piece(1)
    def ring_step(q, hops, turn):
        for way in range(2):
            back_send(q, way, hops, way ^ turn)

    def joint_step(hops):
        for turn in range(2):
            for way in range(2):
                joint_send(way, hops, way ^ 1 ^ turn)

    ring_step(1, 2, 0)
    grad_piece(2)
    ring_step(1, 2, 1)
    hand_across(4, 6)
    ring_step(0, 2, 0)
    grad_piece(3)
    hand_across(6, 8)
    ring_step(1, 1, 0)
    grad_piece(4)
    ring_step(1, 1, 1)
    for c in range(2):
        sums = total(1, c)
        for b in range(2):
            zsend[b, :, pl.ds(*XC[c])] = sums[b].astype(BF)
        z_copy(c, 0).start()
    ring_step(0, 2, 1)
    grad_piece(5)
    across(7, 1).wait_recv()
    for way in range(2):
        joint_send(way, 4, way)
    ring_step(0, 1, 0)
    grad_piece(6)
    for r in (5, 6):
        across(r, 1).wait_recv()
    joint_step(3)
    for c in range(2):
        z_copy(c, 0).wait_recv()
        z_copy(c, 1).start()
    ring_step(0, 1, 1)
    for r in (3, 4):
        across(r, 1).wait_recv()
    joint_step(2)
    for r in (1, 2):
        across(r, 1).wait_recv()
    joint_step(1)
    grad_piece(7)
    across(0, 1).wait_recv()
    for c in range(2):
        sums = total(0, c)
        z_copy(c, 1).wait_recv()
        for b in range(2):
            dt_v[pl.ds(BLK * b, BLK), pl.ds(*XC[c])] = (
                sums[b] + zrecv[b, :, pl.ds(*XC[c])].astype(F32)
            ).astype(BF)
    for c in (1, 0):
        cols = pl.ds(ZC[c][0] - XW, ZC[c][1])
        sums = ours(0, ZC[c])
        for way in range(2):
            joint_copy(way, 1, c).wait_recv()
            sums = plus(sums, [zr[way, 0, b, :, cols].astype(F32) for b in range(2)])
        for b in range(2):
            dt_v[pl.ds(BLK * b, BLK), pl.ds(*ZC[c])] = sums[b].astype(BF)
    outs[3].start()

    for q in range(2):
        for way in range(2):
            for c in range(3):
                gather(q, way, 1, c).wait_send()
                gather(q, way, 2, c).wait_send()
                cut_copy(q, way, c).wait_send()
            gather(q, way, 3, 0).wait_send()
            if way == 0:
                gather(q, way, 4, 0).wait_send()
            last_copy(q, way).wait_send()
            for k in range(4):
                raw_copy(q, way, k).wait_send()
            for hops in (2, 1):
                for c in range(2):
                    back_copy(q, way, hops, c).wait_send()
    for c in range(3):
        for leg in range(2):
            to_mate(c, leg).wait_send()
    each_peer(lambda k: spread(k).wait_send())
    each_peer(lambda k: collect(k).wait_send())
    for c in range(2):
        for leg in range(2):
            z_copy(c, leg).wait_send()
    for r in range(8):
        for leg in range(2):
            across(r, leg).wait_send()
    for way in range(2):
        joint_copy(way, 4, way).wait_send()
        for hops in (3, 2, 1):
            for c in range(2):
                joint_copy(way, hops, c).wait_send()
    for c in outs:
        c.wait()


def hand_out(a, b, c, d, w, x, y, z, va, vb, vc, vd, into, out):
    triples = ((a, va, w), (b, vb, x), (c, vc, y), (d, vd, z))
    parts = []
    for i, (src, mid, dst) in enumerate(triples):
        rows = src.shape[0] // 2
        for j in range(2):
            at = pl.ds(rows * j, rows)
            parts.append((
                pltpu.make_async_copy(src.at[at], mid.at[at], into.at[2 * i + j]),
                pltpu.make_async_copy(mid.at[at], dst.at[at], out.at[2 * i + j]),
            ))
    for first, second in parts:
        first.start()
    for first, second in parts:
        first.wait()
        second.start()
    for first, second in parts:
        second.wait()


def on_device(tokens, grad_out, router_gate, counts, routes, partner, w_gate, w_up, w_down):
    any_ = pl.BlockSpec(memory_space=pl.ANY)
    dma = pltpu.SemaphoreType.DMA
    shape = jax.ShapeDtypeStruct
    outs = pl.pallas_call(
        kernel,
        out_shape=(
            shape((2 * BLK, D), BF), shape((D, H), BF), shape((D, H), BF), shape((H, D), BF),
        ),
        in_specs=[pl.BlockSpec(memory_space=pltpu.SMEM)] * 3 + [any_] * 6,
        out_specs=[any_] * 4,
        scratch_shapes=[
            pltpu.VMEM((4, 2 * BLK), F32),
            pltpu.VMEM((2, 8, GROUP, BLK), F32),
            pltpu.VMEM((2, 5, 2 * BLK, D), BF),
            pltpu.VMEM((2, 5, 2 * BLK, D), BF),
            pltpu.VMEM((16, BLK, D), BF),
            pltpu.VMEM((16, BLK, D), BF),
            pltpu.VMEM((16, BLK, 2 * H), BF),
            pltpu.VMEM((16, BLK, H), BF),
            pltpu.VMEM((16, BLK, D), BF),
            pltpu.VMEM((2, 2, 3, BLK, D), BF),
            pltpu.VMEM((2, 2, BLK, D), BF),
            pltpu.VMEM((2, 2 * BLK, D), BF),
            pltpu.VMEM((GROUP, BLK), F32),
            pltpu.VMEM((2, 2, BLK, XW), BF),
            pltpu.VMEM((2, 2, BLK, XW), BF),
            pltpu.VMEM((2, 2, BLK, XW), BF),
            pltpu.VMEM((2, 2, 2, BLK, XW), BF),
            pltpu.VMEM((2, 2, 2, 2, BLK, XW), BF),
            pltpu.VMEM((2, 2, 2, BLK, D - XW), BF),
            pltpu.VMEM((2, 4, 2, BLK, D - XW), BF),
            pltpu.VMEM((8, BLK, D - XW), BF),
            pltpu.VMEM((8, BLK, D - XW), BF),
            pltpu.VMEM((2, BLK, XW), BF),
            pltpu.VMEM((2, BLK, XW), BF),
            pltpu.VMEM((2, BLK, XW), BF),
            pltpu.VMEM((16, 2, PART, H), BF),
            pltpu.VMEM((NODES, PART, H), BF),
            pltpu.VMEM((NODES, PART, H), BF),
            pltpu.VMEM((NODES, PART, H), BF),
            pltpu.VMEM((D, H), BF),
            pltpu.VMEM((D, H), BF),
            pltpu.VMEM((H, D), BF),
            pltpu.VMEM((2 * BLK, D), BF),
            dma((2, 2, 4, 3)), dma((2, 2, 4, 3)), dma((2, 2, 4)), dma((2, 2, 4)), dma((3, 2)), dma((3, 2)),
            dma((NODES,)), dma((NODES,)), dma((NODES,)), dma((NODES,)),
            dma((2, 2, 4)), dma((2, 2, 4)), dma((2, 2, 2, 2)), dma((2, 2, 2, 2)), dma((2, 4, 2)), dma((2, 4, 2)),
            dma((8, 2)), dma((8, 2)), dma((2, 2)), dma((2, 2)), dma((9,)), dma((4,)),
        ],
        compiler_params=pltpu.CompilerParams(
            collective_id=0, has_side_effects=True, vmem_limit_bytes=67043328
        ),
        name="moe_step",
    )(
        partner, routes.reshape(2, 4), counts, router_gate.T, tokens, grad_out,
        w_gate.reshape(16, 2, 32, H), w_up.reshape(16, 2, 32, H), w_down.reshape(16, 16, D),
    )
    dt, dg, du, dd = pl.pallas_call(
        hand_out,
        out_shape=tuple(shape(o.shape, BF) for o in outs),
        in_specs=[any_] * 4,
        out_specs=[any_] * 4,
        scratch_shapes=[pltpu.VMEM(o.shape, BF) for o in outs] + [dma((8,)), dma((8,))],
        name="hand_out",
    )(*outs)
    return dt, dg.reshape(1, D, H), du.reshape(1, D, H), dd.reshape(1, H, D)


def solution(mesh):
    rows = P(("node", "group"), None)
    cube = P(("node", "group"), None, None)
    return jax.shard_map(
        on_device,
        mesh=mesh,
        in_specs=(rows, rows, rows, P(("node", "group")), cube, P(), cube, cube, cube),
        out_specs=(rows, cube, cube, cube),
        check_vma=False,
    )
```

```python
import functools

import jax
import jax.numpy as jnp
from jax import lax
from jax.experimental import pallas as pl
from jax.experimental.pallas import tpu as pltpu
from jax.sharding import PartitionSpec as P

BF = jnp.bfloat16
F32 = jnp.float32
MESH = pl.DeviceIdType.MESH
NODES = 32
GROUP = 16
RING = 8
BLK = 128
D = 1024
H = 256
XW = 640
XC = ((0, 384), (384, 256))
ZC = ((640, 256), (896, 128))
PART = 96


def slot(hops, way):
    if hops == 0:
        return 0
    return 7 if hops == RING // 2 else 2 * hops - 1 + way


def nt(left, right):
    return lax.dot_general(left, right, (((1,), (1,)), ((), ())), preferred_element_type=F32)


def tn(left, right):
    return lax.dot_general(left, right, (((0,), (0,)), ((), ())), preferred_element_type=F32)


def kernel(
    partner, routes, counts, gates_in, tok_in, gr_in, wg_in, wu_in, wd_in,
    dt_out, dg_out, du_out, dd_out,
    gates, meta, tok, gr, xs, gs, gact, hact, cbuf, cut, relay, zrel, zmeta,
    raw, near, far, sbuf, rbuf, zst, zr, zf, cm, zsend, zl, zrecv,
    pack, mixed, stage, wrec, dg_v, du_v, dd_v, dt_v,
    g_send, g_recv, s_send, s_recv, m_send, m_recv, wa_send, wa_recv, wb_send, wb_recv,
    r_send, r_recv, rs_send, rs_recv, t_send, t_recv, f_send, f_recv, z_send, z_recv, loc, out_sem,
):
    n = lax.axis_index("node")
    me = lax.axis_index("group")
    y = me // 2
    side = me % 2
    ring = (lax.rem(y + 1, RING) * 2 + side, lax.rem(y + RING - 1, RING) * 2 + side)
    mate = y * 2 + (1 - side)
    turned = (n >= NODES // 2).astype(jnp.int32)
    zside = (y * 2 + lax.rem(side + turned, 2), y * 2 + lax.rem(side + 1 - turned, 2))
    beyond = (lax.rem(y + 2, RING) * 2 + side, lax.rem(y + RING - 2, RING) * 2 + side)

    locals_ = [
        pltpu.make_async_copy(wg_in, pack.at[:, :, pl.ds(0, 32), :], loc.at[0]),
        pltpu.make_async_copy(wu_in, pack.at[:, :, pl.ds(32, 32), :], loc.at[1]),
    ]
    for cb in range(4):
        locals_.append(
            pltpu.make_async_copy(
                wd_in.at[:, :, pl.ds(256 * cb, 256)],
                pack.at[:, cb // 2, pl.ds(64 + 16 * (cb % 2), 16), :],
                loc.at[2 + cb],
            )
        )
    owns = [
        pltpu.make_async_copy(gates_in, gates, loc.at[6]),
        pltpu.make_async_copy(tok_in, tok.at[0, 0], loc.at[7]),
        pltpu.make_async_copy(gr_in, gr.at[0, 0], loc.at[8]),
    ]
    for c in owns + locals_:
        c.start()

    barrier = pltpu.get_barrier_semaphore()

    def greet(k, carry):
        pl.semaphore_signal(
            barrier, inc=1, device_id=(lax.rem(n + k, NODES), me), device_id_type=MESH
        )
        return carry

    for g in ring:
        pl.semaphore_signal(barrier, inc=1, device_id=(n, g), device_id_type=MESH)
    lax.fori_loop(1, NODES, greet, 0)
    pl.semaphore_signal(
        barrier, inc=1, device_id=(lax.rem(n + NODES // 2, NODES), mate), device_id_type=MESH
    )

    owns[0].wait()
    device = lax.broadcasted_iota(jnp.int32, (GROUP, BLK), 0)
    table = jnp.zeros((GROUP, BLK), F32)
    for b in range(2):
        for k in range(4):
            asked = jnp.where(b < counts[0], routes[b, k], -1)
            weights = gates[pl.ds(k, 1), pl.ds(BLK * b, BLK)]
            table = jnp.where(device == asked, -weights if b else weights, table)
    meta[0, 0] = table
    pl.semaphore_wait(barrier, NODES - 1 + 3)

    bufs = (meta, tok, gr)
    ins = (meta.at[0, 0], tok_in, gr_in)

    def gather(q, way, hops, c):
        src = ins[c] if q == 0 and hops == 1 else bufs[c].at[q, slot(hops - 1, way)]
        return pltpu.make_async_remote_copy(
            src_ref=src,
            dst_ref=bufs[c].at[q, slot(hops, way)],
            send_sem=g_send.at[q, way, hops - 1, c],
            recv_sem=g_recv.at[q, way, hops - 1, c],
            device_id=(n, ring[way]),
            device_id_type=MESH,
        )

    def cut_copy(q, way, k):
        if k < 2:
            dst = (xs, gs)[k].at[q * 8 + slot(3, way)]
        else:
            dst = relay.at[q, way]
        return pltpu.make_async_remote_copy(
            src_ref=cut.at[q, way, k],
            dst_ref=dst,
            send_sem=s_send.at[q, way, k],
            recv_sem=s_recv.at[q, way, k],
            device_id=(n, ring[way]),
            device_id_type=MESH,
        )

    def last_copy(q, way):
        return pltpu.make_async_remote_copy(
            src_ref=relay.at[q, way],
            dst_ref=(xs, gs)[way].at[q * 8 + 7],
            send_sem=s_send.at[q, way, 3],
            recv_sem=s_recv.at[q, way, 3],
            device_id=(n, ring[way]),
            device_id_type=MESH,
        )

    def to_mate(c, leg):
        stop = zrel.at[c - 1] if c else zmeta
        return pltpu.make_async_remote_copy(
            src_ref=ins[c] if leg == 0 else stop,
            dst_ref=stop if leg == 0 else bufs[c].at[1, 0],
            send_sem=m_send.at[c, leg],
            recv_sem=m_recv.at[c, leg],
            device_id=(lax.rem(n + NODES // 2, NODES), zside[1 if c == 2 else 0]),
            device_id_type=MESH,
        )

    def flip(k):
        return sum(lax.rem(n // (1 << i) + k // (1 << i), 2) * (1 << i) for i in range(5))

    def spread(k):
        to = flip(k)
        return pltpu.make_async_remote_copy(
            src_ref=pack.at[to // 2, lax.rem(to, 2)],
            dst_ref=mixed.at[n],
            send_sem=wa_send.at[k],
            recv_sem=wa_recv.at[k],
            device_id=(to, me),
            device_id_type=MESH,
        )

    def collect(k):
        to = flip(k)
        return pltpu.make_async_remote_copy(
            src_ref=stage.at[to],
            dst_ref=wrec.at[n],
            send_sem=wb_send.at[k],
            recv_sem=wb_recv.at[k],
            device_id=(to, me),
            device_id_type=MESH,
        )

    def each_peer(act):
        def body(k, carry):
            act(k)
            return carry

        lax.fori_loop(1, NODES, body, 0)

    def row_of(q, r, who):
        return (meta[q, r, pl.ds(who, 1), :] < 0.0).astype(F32)

    def choose(q, r, c, who, dst):
        second = row_of(q, r, who)
        first = 1.0 - second
        for cb in range(D // 128):
            cols = pl.ds(128 * cb, 128)
            a = bufs[c][q, r, pl.ds(0, BLK), cols].astype(F32)
            b = bufs[c][q, r, pl.ds(BLK, BLK), cols].astype(F32)
            dst[:, cols] = (a * first + b * second).astype(BF)

    def arrive(q, hops, c):
        if hops == 1:
            for way in range(2):
                gather(q, way, 1, c).wait_recv()
                gather(q, way, 2, c).start()
        elif hops == 2:
            for way in range(2):
                gather(q, way, 2, c).wait_recv()
                if c == 0:
                    gather(q, way, 3, 0).start()
                    continue
                if c == 1 + way:
                    choose(q, slot(2, way), c, beyond[way], cut.at[q, way, 2])
                    cut_copy(q, way, 2).start()
                choose(q, slot(2, way), c, ring[way], cut.at[q, way, c - 1])
                cut_copy(q, way, c - 1).start()
        elif hops == 3:
            for way in range(2):
                if c == 0:
                    gather(q, way, 3, 0).wait_recv()
                    if way == 0:
                        gather(q, way, 4, 0).start()
                    continue
                if c == 1 + way:
                    cut_copy(q, way, 2).wait_recv()
                    last_copy(q, way).start()
                cut_copy(q, way, c - 1).wait_recv()
        elif c == 0:
            gather(q, 0, 4, 0).wait_recv()
        else:
            last_copy(q, c - 1).wait_recv()

    pick_me = (lax.broadcasted_iota(jnp.int32, (GROUP, 128), 0) == me).astype(F32)

    def compute(pair, carry):
        two = pl.ds(2 * pair, 2)
        x = xs[two].reshape(2 * BLK, D)
        wg = wrec[:, pl.ds(0, 32), :].reshape(D, H)
        wu = wrec[:, pl.ds(32, 32), :].reshape(D, H)
        gate_pre = jnp.dot(x, wg, preferred_element_type=F32)
        up_pre = jnp.dot(x, wu, preferred_element_type=F32)
        grad_hidden = None
        for cb in range(4):
            g = gs[two, :, pl.ds(256 * cb, 256)].reshape(2 * BLK, 256)
            w = wd_block(cb)
            term = nt(g, w)
            grad_hidden = term if grad_hidden is None else grad_hidden + term
        weight = jnp.concatenate(
            [
                lax.dot_general(
                    meta[pair // 4, 2 * lax.rem(pair, 4) + j], pick_me, (((0,), (0,)), ((), ())),
                    preferred_element_type=F32, precision=lax.Precision.HIGHEST,
                )
                for j in range(2)
            ],
            axis=0,
        )
        weight = jnp.abs(jnp.concatenate([weight, weight], axis=1))
        sig = 1.0 / (1.0 + jnp.exp(-gate_pre))
        swish = gate_pre * sig
        grad_hidden = grad_hidden * weight
        hact[two] = (swish * up_pre * weight).astype(BF).reshape(2, BLK, H)
        gu = (grad_hidden * swish).astype(BF)
        gg = (grad_hidden * up_pre * sig * (1.0 + gate_pre * (1.0 - sig))).astype(BF)
        gact[two, :, pl.ds(0, H)] = gg.reshape(2, BLK, H)
        gact[two, :, pl.ds(H, H)] = gu.reshape(2, BLK, H)
        back = nt(gg, wg) + nt(gu, wu)
        cbuf[two] = back.astype(BF).reshape(2, BLK, D)
        return carry

    def wd_block(cb):
        rows = pl.ds(64 + 16 * (cb % 2), 16)
        parts = [wrec[2 * i + cb // 2, rows, :] for i in range(16)]
        return jnp.concatenate(parts, axis=0)

    def run(first, last):
        lax.fori_loop(first, last, compute, 0)

    def pick(q, first, last):
        def body(r, carry):
            for c, sel in ((1, xs), (2, gs)):
                choose(q, r, c, me, sel.at[q * 8 + r])
            return carry

        lax.fori_loop(first, last, body, 0)

    def raw_copy(q, way, k):
        cols = pl.ds(*XC[k if k < 2 else way])
        if k == 2:
            src, dst = cbuf.at[q * 8 + 7, :, cols], near.at[q, way, :, cols]
        elif k == 3:
            src, dst = near.at[q, way, :, cols], far.at[q, way, :, cols]
        else:
            src, dst = cbuf.at[q * 8 + slot(3, 1 - way), :, cols], raw.at[q, way, :, cols]
        return pltpu.make_async_remote_copy(
            src_ref=src,
            dst_ref=dst,
            send_sem=r_send.at[q, way, k],
            recv_sem=r_recv.at[q, way, k],
            device_id=(n, ring[way]),
            device_id_type=MESH,
        )

    def across(r, leg):
        return pltpu.make_async_remote_copy(
            src_ref=zf.at[r] if leg else cbuf.at[8 + r, :, pl.ds(XW, D - XW)],
            dst_ref=cm.at[r] if leg else zf.at[r],
            send_sem=f_send.at[r, leg],
            recv_sem=f_recv.at[r, leg],
            device_id=(lax.rem(n + NODES // 2, NODES), zside[r % 2]),
            device_id_type=MESH,
        )

    def hand_across(first, last):
        for r in range(first, last):
            across(r, 0).wait_recv()
            across(r, 1).start()

    for c in range(3):
        for way in range(2):
            gather(0, way, 1, c).start()
    for c in range(3):
        to_mate(c, 0).start()
    for c in locals_:
        c.wait()
    mixed[n] = pack[n // 2, lax.rem(n, 2)]
    for c in owns[1:]:
        c.wait()
    pick(0, 0, 1)
    for c in range(2):
        arrive(0, 1, c)
    for c in range(2):
        to_mate(c, 0).wait_recv()
        to_mate(c, 1).start()
    arrive(0, 1, 2)
    to_mate(2, 0).wait_recv()
    to_mate(2, 1).start()
    each_peer(lambda k: spread(k).start())
    pick(0, 1, 3)
    for c in range(3):
        arrive(0, 2, c)
    pick(0, 3, 5)
    for c in range(2):
        arrive(0, 3, c)
    for c in range(2):
        to_mate(c, 1).wait_recv()
        for way in range(2):
            gather(1, way, 1, c).start()
    arrive(0, 3, 2)
    to_mate(2, 1).wait_recv()
    for way in range(2):
        gather(1, way, 1, 2).start()
    pick(1, 0, 1)
    for c in range(3):
        arrive(0, 4, c)
    each_peer(lambda k: spread(k).wait_recv())

    def forward(k):
        to = flip(k)
        stage[to] = mixed[partner[to]]
        collect(k).start()

    each_peer(forward)
    wrec[n] = mixed[partner[n]]
    for c in range(3):
        arrive(1, 1, c)
    pick(1, 1, 3)
    for c in range(3):
        arrive(1, 2, c)
    pick(1, 3, 5)
    each_peer(lambda k: collect(k).wait_recv())
    run(4, 6)
    for r in range(4):
        across(r, 0).start()
    for c in range(2):
        arrive(1, 3, c)
    run(0, 2)
    arrive(1, 3, 2)
    run(2, 4)
    for way in range(2):
        for k in (2, 0, 1):
            raw_copy(0, way, k).start()
    run(6, 7)
    for r in range(4, 6):
        across(r, 0).start()
    hand_across(0, 4)
    for c in range(3):
        arrive(1, 4, c)
    run(7, 8)

    outs = [
        pltpu.make_async_copy(dg_v, dg_out, out_sem.at[0]),
        pltpu.make_async_copy(du_v, du_out, out_sem.at[1]),
        pltpu.make_async_copy(dd_v, dd_out, out_sem.at[2]),
        pltpu.make_async_copy(dt_v, dt_out, out_sem.at[3]),
    ]

    def grad_piece(i):
        cols = pl.ds(256 * (i % 4), 256)
        if i < 4:
            x = xs[:, :, cols].reshape(GROUP * BLK, 256)
            both = tn(x, gact[...].reshape(GROUP * BLK, 2 * H))
            dg_v[cols, :] = both[:, :H].astype(BF)
            du_v[cols, :] = both[:, H:].astype(BF)
        else:
            g = gs[:, :, cols].reshape(GROUP * BLK, 256)
            dd_v[:, cols] = tn(hact[...].reshape(GROUP * BLK, H), g).astype(BF)
        if i == 3:
            outs[0].start()
            outs[1].start()
        if i == 7:
            outs[2].start()

    def placed(block, row):
        second = jnp.concatenate([row] * (block.shape[1] // 128), axis=1)
        block = block.astype(F32)
        return [block * (1.0 - second), block * second]

    def plus(left, right):
        return [u + v for u, v in zip(left, right)]

    def mine(q, r, cols):
        return placed(cbuf[q * 8 + r, :, pl.ds(*cols)], row_of(q, r, me))

    def ours(r, cols):
        other = placed(cm[r, :, pl.ds(cols[0] - XW, cols[1])], row_of(0, r, mate))
        return plus(mine(0, r, cols), other)

    def back_copy(q, way, hops, c):
        cols = pl.ds(*XC[c])
        return pltpu.make_async_remote_copy(
            src_ref=sbuf.at[q, way, :, :, cols] if hops == 2 else rbuf.at[q, way, 1, :, :, cols],
            dst_ref=rbuf.at[q, way, hops - 1, :, :, cols],
            send_sem=rs_send.at[q, way, hops - 1, c],
            recv_sem=rs_recv.at[q, way, hops - 1, c],
            device_id=(n, ring[way]),
            device_id_type=MESH,
        )

    def back_send(q, way, hops, c):
        r = slot(hops, 1 - way)
        cols = pl.ds(*XC[c])
        sums = mine(q, r, XC[c])
        if hops == 2:
            raw_copy(q, way, c).wait_recv()
            sums = plus(sums, placed(raw[q, way, :, cols], row_of(q, r, ring[1 - way])))
            if c == way:
                raw_copy(q, way, 3).wait_recv()
                sums = plus(sums, placed(far[q, way, :, cols], row_of(q, r, beyond[1 - way])))
            for b in range(2):
                sbuf[q, way, b, :, cols] = sums[b].astype(BF)
        else:
            back_copy(q, way, 2, c).wait_recv()
            for b in range(2):
                rbuf[q, way, 1, b, :, cols] = (
                    rbuf[q, way, 1, b, :, cols].astype(F32) + sums[b]
                ).astype(BF)
        back_copy(q, way, hops, c).start()

    def total(q, c):
        cols = pl.ds(*XC[c])
        sums = mine(q, 0, XC[c])
        for way in range(2):
            back_copy(q, way, 1, c).wait_recv()
            sums = plus(sums, [rbuf[q, way, 0, b, :, cols].astype(F32) for b in range(2)])
        return sums

    def joint_copy(way, hops, c):
        cols = pl.ds(ZC[c][0] - XW, ZC[c][1])
        fresh = hops == 4 or (hops == 3 and c == way)
        return pltpu.make_async_remote_copy(
            src_ref=zst.at[way, 4 - hops, :, :, cols] if fresh else zr.at[way, hops, :, :, cols],
            dst_ref=zr.at[way, hops - 1, :, :, cols],
            send_sem=t_send.at[way, hops - 1, c],
            recv_sem=t_recv.at[way, hops - 1, c],
            device_id=(n, ring[way]),
            device_id_type=MESH,
        )

    def joint_send(way, hops, c):
        cols = pl.ds(ZC[c][0] - XW, ZC[c][1])
        sums = ours(slot(hops, 1 - way), ZC[c])
        if hops == 4 or (hops == 3 and c == way):
            for b in range(2):
                zst[way, 4 - hops, b, :, cols] = sums[b].astype(BF)
        else:
            joint_copy(way, hops + 1, c).wait_recv()
            for b in range(2):
                zr[way, hops, b, :, cols] = (
                    zr[way, hops, b, :, cols].astype(F32) + sums[b]
                ).astype(BF)
        joint_copy(way, hops, c).start()

    def z_copy(c, leg):
        cols = pl.ds(*XC[c])
        return pltpu.make_async_remote_copy(
            src_ref=zl.at[:, :, cols] if leg else zsend.at[:, :, cols],
            dst_ref=zrecv.at[:, :, cols] if leg else zl.at[:, :, cols],
            send_sem=z_send.at[c, leg],
            recv_sem=z_recv.at[c, leg],
            device_id=(lax.rem(n + NODES // 2, NODES), zside[c]),
            device_id_type=MESH,
        )

    for way in range(2):
        for k in (2, 0, 1):
            raw_copy(1, way, k).start()
    for r in range(6, 8):
        across(r, 0).start()
    grad_piece(0)
    for q in (1, 0):
        for way in range(2):
            raw_copy(q, way, 2).wait_recv()
            raw_copy(q, way, 3).start()
    grad_piece(1)
    def ring_step(q, hops, turn):
        for way in range(2):
            back_send(q, way, hops, way ^ turn)

    def joint_step(hops):
        for turn in range(2):
            for way in range(2):
                joint_send(way, hops, way ^ turn)

    ring_step(1, 2, 0)
    grad_piece(2)
    ring_step(1, 2, 1)
    hand_across(4, 6)
    ring_step(0, 2, 0)
    grad_piece(3)
    hand_across(6, 8)
    ring_step(1, 1, 0)
    grad_piece(4)
    ring_step(1, 1, 1)
    for c in range(2):
        sums = total(1, c)
        for b in range(2):
            zsend[b, :, pl.ds(*XC[c])] = sums[b].astype(BF)
        z_copy(c, 0).start()
    ring_step(0, 2, 1)
    grad_piece(5)
    across(7, 1).wait_recv()
    for way in range(2):
        joint_send(way, 4, 1 - way)
    ring_step(0, 1, 0)
    grad_piece(6)
    for r in (5, 6):
        across(r, 1).wait_recv()
    joint_step(3)
    for c in range(2):
        z_copy(c, 0).wait_recv()
        z_copy(c, 1).start()
    ring_step(0, 1, 1)
    for r in (3, 4):
        across(r, 1).wait_recv()
    joint_step(2)
    for r in (1, 2):
        across(r, 1).wait_recv()
    joint_step(1)
    grad_piece(7)
    across(0, 1).wait_recv()
    for c in range(2):
        sums = total(0, c)
        z_copy(c, 1).wait_recv()
        for b in range(2):
            dt_v[pl.ds(BLK * b, BLK), pl.ds(*XC[c])] = (
                sums[b] + zrecv[b, :, pl.ds(*XC[c])].astype(F32)
            ).astype(BF)
    for c in (1, 0):
        cols = pl.ds(ZC[c][0] - XW, ZC[c][1])
        sums = ours(0, ZC[c])
        for way in range(2):
            joint_copy(way, 1, c).wait_recv()
            sums = plus(sums, [zr[way, 0, b, :, cols].astype(F32) for b in range(2)])
        for b in range(2):
            dt_v[pl.ds(BLK * b, BLK), pl.ds(*ZC[c])] = sums[b].astype(BF)
    outs[3].start()

    for q in range(2):
        for way in range(2):
            for c in range(3):
                gather(q, way, 1, c).wait_send()
                gather(q, way, 2, c).wait_send()
                cut_copy(q, way, c).wait_send()
            gather(q, way, 3, 0).wait_send()
            if way == 0:
                gather(q, way, 4, 0).wait_send()
            last_copy(q, way).wait_send()
            for k in range(4):
                raw_copy(q, way, k).wait_send()
            for hops in (2, 1):
                for c in range(2):
                    back_copy(q, way, hops, c).wait_send()
    for c in range(3):
        for leg in range(2):
            to_mate(c, leg).wait_send()
    each_peer(lambda k: spread(k).wait_send())
    each_peer(lambda k: collect(k).wait_send())
    for c in range(2):
        for leg in range(2):
            z_copy(c, leg).wait_send()
    for r in range(8):
        for leg in range(2):
            across(r, leg).wait_send()
    for way in range(2):
        joint_copy(way, 4, 1 - way).wait_send()
        for hops in (3, 2, 1):
            for c in range(2):
                joint_copy(way, hops, c).wait_send()
    for c in outs:
        c.wait()


def hand_out(a, b, c, d, w, x, y, z, va, vb, vc, vd, into, out):
    triples = ((a, va, w), (b, vb, x), (c, vc, y), (d, vd, z))
    parts = []
    for i, (src, mid, dst) in enumerate(triples):
        rows = src.shape[0] // 2
        for j in range(2):
            at = pl.ds(rows * j, rows)
            parts.append((
                pltpu.make_async_copy(src.at[at], mid.at[at], into.at[2 * i + j]),
                pltpu.make_async_copy(mid.at[at], dst.at[at], out.at[2 * i + j]),
            ))
    for first, second in parts:
        first.start()
    for first, second in parts:
        first.wait()
        second.start()
    for first, second in parts:
        second.wait()


def on_device(tokens, grad_out, router_gate, counts, routes, partner, w_gate, w_up, w_down):
    any_ = pl.BlockSpec(memory_space=pl.ANY)
    dma = pltpu.SemaphoreType.DMA
    shape = jax.ShapeDtypeStruct
    outs = pl.pallas_call(
        kernel,
        out_shape=(
            shape((2 * BLK, D), BF), shape((D, H), BF), shape((D, H), BF), shape((H, D), BF),
        ),
        in_specs=[pl.BlockSpec(memory_space=pltpu.SMEM)] * 3 + [any_] * 6,
        out_specs=[any_] * 4,
        scratch_shapes=[
            pltpu.VMEM((4, 2 * BLK), F32),
            pltpu.VMEM((2, 8, GROUP, BLK), F32),
            pltpu.VMEM((2, 5, 2 * BLK, D), BF),
            pltpu.VMEM((2, 5, 2 * BLK, D), BF),
            pltpu.VMEM((16, BLK, D), BF),
            pltpu.VMEM((16, BLK, D), BF),
            pltpu.VMEM((16, BLK, 2 * H), BF),
            pltpu.VMEM((16, BLK, H), BF),
            pltpu.VMEM((16, BLK, D), BF),
            pltpu.VMEM((2, 2, 3, BLK, D), BF),
            pltpu.VMEM((2, 2, BLK, D), BF),
            pltpu.VMEM((2, 2 * BLK, D), BF),
            pltpu.VMEM((GROUP, BLK), F32),
            pltpu.VMEM((2, 2, BLK, XW), BF),
            pltpu.VMEM((2, 2, BLK, XW), BF),
            pltpu.VMEM((2, 2, BLK, XW), BF),
            pltpu.VMEM((2, 2, 2, BLK, XW), BF),
            pltpu.VMEM((2, 2, 2, 2, BLK, XW), BF),
            pltpu.VMEM((2, 2, 2, BLK, D - XW), BF),
            pltpu.VMEM((2, 4, 2, BLK, D - XW), BF),
            pltpu.VMEM((8, BLK, D - XW), BF),
            pltpu.VMEM((8, BLK, D - XW), BF),
            pltpu.VMEM((2, BLK, XW), BF),
            pltpu.VMEM((2, BLK, XW), BF),
            pltpu.VMEM((2, BLK, XW), BF),
            pltpu.VMEM((16, 2, PART, H), BF),
            pltpu.VMEM((NODES, PART, H), BF),
            pltpu.VMEM((NODES, PART, H), BF),
            pltpu.VMEM((NODES, PART, H), BF),
            pltpu.VMEM((D, H), BF),
            pltpu.VMEM((D, H), BF),
            pltpu.VMEM((H, D), BF),
            pltpu.VMEM((2 * BLK, D), BF),
            dma((2, 2, 4, 3)), dma((2, 2, 4, 3)), dma((2, 2, 4)), dma((2, 2, 4)), dma((3, 2)), dma((3, 2)),
            dma((NODES,)), dma((NODES,)), dma((NODES,)), dma((NODES,)),
            dma((2, 2, 4)), dma((2, 2, 4)), dma((2, 2, 2, 2)), dma((2, 2, 2, 2)), dma((2, 4, 2)), dma((2, 4, 2)),
            dma((8, 2)), dma((8, 2)), dma((2, 2)), dma((2, 2)), dma((9,)), dma((4,)),
        ],
        compiler_params=pltpu.CompilerParams(
            collective_id=0, has_side_effects=True, vmem_limit_bytes=67043328
        ),
        name="moe_step",
    )(
        partner, routes.reshape(2, 4), counts, router_gate.T, tokens, grad_out,
        w_gate.reshape(16, 2, 32, H), w_up.reshape(16, 2, 32, H), w_down.reshape(16, 16, D),
    )
    dt, dg, du, dd = pl.pallas_call(
        hand_out,
        out_shape=tuple(shape(o.shape, BF) for o in outs),
        in_specs=[any_] * 4,
        out_specs=[any_] * 4,
        scratch_shapes=[pltpu.VMEM(o.shape, BF) for o in outs] + [dma((8,)), dma((8,))],
        name="hand_out",
    )(*outs)
    return dt, dg.reshape(1, D, H), du.reshape(1, D, H), dd.reshape(1, H, D)


def solution(mesh):
    rows = P(("node", "group"), None)
    cube = P(("node", "group"), None, None)
    return jax.shard_map(
        on_device,
        mesh=mesh,
        in_specs=(rows, rows, rows, P(("node", "group")), cube, P(), cube, cube, cube),
        out_specs=(rows, cube, cube, cube),
        check_vma=False,
    )
```
